128 devices in a mesh: dp: 8 (over y, core), tm: 16 (over z, x).
Axes of the slice: x: 4, y: 4, z: 4, core: 2. Of those that a mesh axis runs over, the one named last changes fastest.
Arguments:
- grad_out: float32 [8, 16384, 512], P('dp', 'tm'), may hold values from -6 to 6
- input_spectrum: float32 [2, 8, 2, 16, 1024, 512], P(None, 'dp', None, 'tm'), may hold values from -6 to 6
- filter_spectrum: float32 [2, 2, 16, 1024, 512], P(None, None, 'tm'), may hold values from -6 to 6
- skip_gain: float32 [512], replicated, may hold values from 0.5 to 2
Outputs:
- grad_in: float32 [8, 16384, 512], P('dp', 'tm')
- grad_filter: float32 [2, 2, 16, 1024, 512], P(None, None, 'tm', 'dp')
The draws below stay inside these ranges and needn't reach their ends.
All inputs are finite; a program needn't handle non-finite values.
Results may differ from the reference program's by a relative error of at most 0.0001.
Values sent between devices are 32-bit elements; how exact they have to be, the bound alone decides.
No kernel may reach another device: no remote copies, remote signals or barrier semaphores. Data moves between devices by JAX's collectives and lax.ppermute only.
A program may use at most 192 MiB of HBM per device.

```python
import math
import jax
import jax.numpy as jnp
from jax import lax

C = 512
L_DEV = 1024
STREAMS = 8
STEPS = 16384
RES = 16


def block_levels(rng, dims, cuts, least, top_value):
    factor_of = 1.0
    for axis_at, blocks in cuts:
        draws = jax.random.uniform(jax.random.fold_in(jax.random.fold_in(rng, 6), axis_at), (blocks,), jnp.float32, least / len(cuts), top_value / len(cuts))
        factor_of = factor_of * jnp.repeat(jnp.exp(draws), dims[axis_at] // blocks).reshape((-1,) + (1,) * (len(dims) - 1 - axis_at))
    return factor_of


def centred(stream_key, extent, width, limit, pieces=(), kind=jnp.bfloat16):
    result = jax.random.normal(stream_key, extent, jnp.float32) * width
    if len(pieces) > 0:
        result = block_levels(stream_key, extent, pieces, -0.22, 0.18) * result
    return jnp.clip(result, min=-limit, max=limit).astype(kind)


def setup_inputs(seed: int = 0) -> dict:
    key_of = jax.random.split(jax.random.key(seed), 5)
    return {
        "grad_out": centred(key_of[0], (STREAMS, STEPS, C), 1.0, 6.0, ((0, 8), (1, 16)), jnp.float32),
        "input_spectrum": centred(key_of[1], (2, STREAMS, 2, RES, L_DEV, C), 1.0, 6.0, ((1, 8), (3, 16)), jnp.float32),
        "filter_spectrum": centred(key_of[2], (2, 2, RES, L_DEV, C), 1.0, 6.0, ((2, 16),), jnp.float32),
        "skip_gain": jnp.clip(jax.random.uniform(key_of[3], (C,), jnp.float32, 0.5, 2.0), 0.5, 2.0),
    }


def reference(grad_out, input_spectrum, filter_spectrum, skip_gain):
    points = 2 * STEPS
    factor = 1.0 / math.sqrt(points)

    def layout(spectrum):
        arranged = spectrum.reshape(L_DEV, RES, 2, C).transpose(2, 1, 0, 3)
        return (jnp.real(arranged), jnp.imag(arranged))

    def unlayout(real_part, imag_part):
        arranged = lax.complex(real_part, imag_part)
        return arranged.transpose(2, 1, 0, 3).reshape(points, C)

    def per_stream(running, element):
        signal, saved = element
        padded = jnp.concatenate([signal, jnp.zeros_like(signal)], 0)
        spec_real, spec_imag = layout(jnp.fft.fft(padded, axis=0) * factor)
        saved_real, saved_imag = (saved[0], saved[1])
        term_real = saved_real * spec_real + saved_imag * spec_imag
        term_imag = saved_real * spec_imag - saved_imag * spec_real
        running = running + jnp.stack([term_real, term_imag])
        filt_real, filt_imag = (filter_spectrum[0], filter_spectrum[1])
        grad_real = filt_real * spec_real + filt_imag * spec_imag
        grad_imag = filt_real * spec_imag - filt_imag * spec_real
        restored = jnp.fft.ifft(unlayout(grad_real, grad_imag), axis=0) * (points * factor)
        grad_row = jnp.real(restored[:STEPS]) + skip_gain * signal
        return (running, grad_row)
    initial = jnp.zeros((2, 2, RES, L_DEV, C), jnp.float32)
    grad_filter, grad_in = lax.scan(per_stream, initial, (grad_out, jnp.moveaxis(input_spectrum, 1, 0)))
    return (grad_in, grad_filter)
```

```python
import functools
import math

import jax
import jax.numpy as jnp
from jax import lax
from jax.experimental import pallas as pl
from jax.experimental.pallas import tpu as pltpu
from jax.sharding import PartitionSpec as P

LANES = 128
SHARDS = 16
RADIX = 4


def weighted(pairs):
    total = None
    for coefficient, value in pairs:
        if abs(coefficient) < 1e-12:
            continue
        if total is None:
            if abs(coefficient - 1.0) < 1e-12:
                total = value
            else:
                total = value * coefficient
        elif abs(coefficient - 1.0) < 1e-12:
            total = total + value
        elif abs(coefficient + 1.0) < 1e-12:
            total = total - value
        else:
            total = total + value * coefficient
    return total


def cos_at(numerator, denominator):
    return math.cos(2.0 * math.pi * (numerator % denominator) / denominator)


def sin_at(numerator, denominator):
    return math.sin(2.0 * math.pi * (numerator % denominator) / denominator)


def residues_of(x):
    total = {n: x[n] + x[16 - n] for n in range(1, 8)}
    diff = {n: x[n] - x[16 - n] for n in range(1, 8)}
    out = {}
    evens, odds = (2, 4, 6), (1, 3, 5, 7)
    for a in range(0, 5):
        even_re = weighted([(1.0, x[0]), (cos_at(8 * a, 16), x[8])] + [(cos_at(n * a, 16), total[n]) for n in evens])
        odd_re = weighted([(cos_at(n * a, 16), total[n]) for n in odds])
        even_im = weighted([(sin_at(n * a, 16), diff[n]) for n in evens])
        odd_im = weighted([(sin_at(n * a, 16), diff[n]) for n in odds])
        if a == 4:
            out[2 * a] = (even_re, -odd_im)
            continue
        re_low, re_high = even_re + odd_re, even_re - odd_re
        if a == 0:
            out[0], out[16] = (re_low, None), (re_high, None)
        else:
            out[2 * a] = (re_low, -(even_im + odd_im))
            out[16 - 2 * a] = (re_high, even_im - odd_im)
    for rho in (1, 3, 5, 7):
        even_re = weighted([(1.0, x[0])] + [(cos_at(n * rho, 32), diff[n]) for n in evens])
        odd_re = weighted([(cos_at(n * rho, 32), diff[n]) for n in odds])
        even_im = weighted([(sin_at(8 * rho, 32), x[8])] + [(sin_at(n * rho, 32), total[n]) for n in evens])
        odd_im = weighted([(sin_at(n * rho, 32), total[n]) for n in odds])
        out[rho] = (even_re + odd_re, -(even_im + odd_im))
        out[16 - rho] = (even_re - odd_re, even_im - odd_im)
    return out


def expand_kernel(x_ref, out_ref):
    groups = x_ref.shape[1] // RADIX // 8

    def step(index, carry):
        t, group = index // groups, index % groups
        row = pl.ds(pl.multiple_of(group * 8, 8), 8)
        values = [x_ref[n, pl.ds(group * 8 * RADIX + t, 8, stride=RADIX), :] for n in range(SHARDS)]
        found = residues_of(values)
        zero = jnp.zeros_like(values[0])
        for a in range(SHARDS):
            even, odd = 2 * a, 2 * a + 1
            if even <= 16:
                re, im = found[even]
                if a == 0:
                    im = found[16][0]
                elif a == 8:
                    im = zero
            else:
                re, im = found[32 - even]
                im = -im
            out_ref[a, 0, t, row, :] = re
            out_ref[a, 1, t, row, :] = im
            if odd <= 16:
                re, im = found[odd]
            else:
                re, im = found[32 - odd]
                im = -im
            out_ref[a, 2, t, row, :] = re
            out_ref[a, 3, t, row, :] = im
        return carry

    lax.fori_loop(0, RADIX * groups, step, 0)


def times_of(v0, v16, even, odd):
    out = [None] * 16
    ce, se, co, so = {}, {}, {}, {}
    for n in range(0, 5):
        c_even = weighted([(1.0, v0), (1.0 if n % 2 == 0 else -1.0, v16)] + [(cos_at(n * d, 16), even[d][0]) for d in (2, 4, 6)])
        c_odd = weighted([(cos_at(n * d, 16), even[d][0]) for d in (1, 3, 5, 7)])
        s_even = weighted([(sin_at(n * d, 16), even[d][1]) for d in (2, 4, 6)])
        s_odd = weighted([(sin_at(n * d, 16), even[d][1]) for d in (1, 3, 5, 7)])
        if n == 4:
            ce[4], se[4] = c_even, s_odd
        elif n == 0:
            ce[0], ce[8] = c_even + c_odd, c_even - c_odd
        else:
            ce[n], ce[8 - n] = c_even + c_odd, c_even - c_odd
            se[n], se[8 - n] = s_odd + s_even, s_odd - s_even
    re_sum = {q: odd[q][0] + odd[16 - q][0] for q in (1, 3, 5, 7)}
    re_diff = {q: odd[q][0] - odd[16 - q][0] for q in (1, 3, 5, 7)}
    im_sum = {q: odd[q][1] + odd[16 - q][1] for q in (1, 3, 5, 7)}
    im_diff = {q: odd[q][1] - odd[16 - q][1] for q in (1, 3, 5, 7)}
    for n in range(0, 9):
        re_of, im_of = (re_sum, im_diff) if n % 2 == 0 else (re_diff, im_sum)
        co[n] = weighted([(cos_at(n * q, 32), re_of[q]) for q in (1, 3, 5, 7)])
        so[n] = weighted([(sin_at(n * q, 32), im_of[q]) for q in (1, 3, 5, 7)])
    out[0] = ce[0] + co[0]
    out[8] = ce[8] + so[8]
    for n in range(1, 8):
        out[n] = (ce[n] - se[n]) + (co[n] + so[n])
        out[16 - n] = (ce[n] + se[n]) + (so[n] - co[n])
    return out


def combine_kernel(u_ref, x_ref, gain_ref, out_ref):
    groups = x_ref.shape[1] // RADIX // 8

    def step(index, carry):
        t, group = index // groups, index % groups
        row = pl.ds(pl.multiple_of(group * 8, 8), 8)
        even = {d: (u_ref[d, 0, t, row, :], u_ref[d, 1, t, row, :]) for d in range(1, 8)}
        odd = {31 - 2 * d: (u_ref[d, 0, t, row, :], u_ref[d, 1, t, row, :]) for d in range(8, 16)}
        times = times_of(u_ref[0, 0, t, row, :], u_ref[0, 1, t, row, :], even, odd)
        gain = gain_ref[0:1, :]
        rows = pl.ds(group * 8 * RADIX + t, 8, stride=RADIX)
        for n in range(SHARDS):
            out_ref[n, rows, :] = times[n] + gain * x_ref[n, rows, :]
        return carry

    lax.fori_loop(0, RADIX * groups, step, 0)


def halves_of(values):
    high = values.astype(jnp.bfloat16)
    low = (values - high.astype(jnp.float32)).astype(jnp.bfloat16)
    return high, low


def product(table_ref, where, values):
    high, low = halves_of(values)
    table_high = table_ref[where + (0,)]
    table_low = table_ref[where + (1,)]
    dot = functools.partial(jnp.dot, preferred_element_type=jnp.float32)
    return dot(table_high, high) + (dot(table_high, low) + dot(table_low, high))


def spectrum_kernel(pick_ref, z_ref, saved_ref, filt_ref, mirror_ref, fwd_ref, inv_ref, fwd16_ref, inv16_ref, term_ref, u_ref, s_ref, h_ref):
    pick = pick_ref[0]
    first = pick_ref[1]
    keep = (1 - first).astype(jnp.float32)
    inner = fwd_ref.shape[-1]
    lanes = z_ref.shape[-1]

    def turn(parts, sign):
        (r0, i0), (r1, i1), (r2, i2), (r3, i3) = parts
        ar, ai, br, bi = r0 + r2, i0 + i2, r0 - r2, i0 - i2
        cr, ci, dr, di = r1 + r3, i1 + i3, r1 - r3, i1 - i3
        if sign < 0:
            dr, di = -dr, -di
        return (ar + cr, ai + ci), (br + di, bi - dr), (ar - cr, ai - ci), (br - di, bi + dr)

    for r in range(2):
        for t in range(RADIX):
            re = z_ref[:, 2 * r, t].reshape(inner, lanes)
            im = z_ref[:, 2 * r + 1, t].reshape(inner, lanes)
            if r == 0:
                im = im * keep
            both = product(fwd_ref, (r, t), jnp.concatenate([re, im], 1))
            s_ref[r, t, 0] = both[:inner, :lanes] + both[inner:, lanes:]
            s_ref[r, t, 1] = both[:inner, lanes:] - both[inner:, :lanes]

        def rows_step(index, carry):
            row = pl.ds(pl.multiple_of(index * 8, 8), 8)
            parts = [(s_ref[r, t, 0, row], s_ref[r, t, 1, row]) for t in range(RADIX)]
            for q, (re, im) in enumerate(turn(parts, 1)):
                s_ref[r, q, 0, row] = re
                s_ref[r, q, 1, row] = im
                at = pl.ds(pl.multiple_of(q * inner + index * 8, 8), 8)
                a, b = saved_ref[0, r, at], saved_ref[1, r, at]
                term_ref[0, r, at] = a * re + b * im
                term_ref[1, r, at] = a * im - b * re
            return carry

        lax.fori_loop(0, inner // 8, rows_step, 0, unroll=2)

    def back_step(index, carry):
        row = pl.ds(pl.multiple_of(index * 8, 8), 8)
        parts = []
        for q in range(RADIX):
            at = pl.ds(pl.multiple_of(q * inner + index * 8, 8), 8)
            a = filt_ref[0, at] + keep * mirror_ref[0, at]
            b = keep * mirror_ref[1, at] - filt_ref[1, at]
            re, im = s_ref[pick, q, 0, row], s_ref[pick, q, 1, row]
            parts.append((a * re - b * im, a * im + b * re))
        for t, (re, im) in enumerate(turn(parts, -1)):
            h_ref[t, 0, row] = re
            h_ref[t, 1, row] = im
        return carry

    lax.fori_loop(0, inner // 8, back_step, 0, unroll=2)
    slivers = u_ref.shape[0]
    for t in range(RADIX):
        both = product(inv_ref, (t,), jnp.concatenate([h_ref[t, 0], h_ref[t, 1]], 1))
        u_ref[:, 0, t] = (both[:inner, :lanes] - both[inner:, lanes:]).reshape(slivers, inner // slivers, lanes)
        u_ref[:, 1, t] = (both[inner:, :lanes] + both[:inner, lanes:]).reshape(slivers, inner // slivers, lanes)

    @pl.when(first == 1)
    def _():
        for t in range(RADIX):
            both = product(fwd16_ref, (t,), z_ref[:, 1, t].reshape(inner, lanes))
            s_ref[1, t, 0] = both[:inner]
            s_ref[1, t, 1] = -both[inner:]

        def step16(index, carry):
            row = pl.ds(pl.multiple_of(index * 8, 8), 8)
            parts = []
            for q, (re, im) in enumerate(turn([(s_ref[1, t, 0, row], s_ref[1, t, 1, row]) for t in range(RADIX)], 1)):
                at = pl.ds(pl.multiple_of(q * inner + index * 8, 8), 8)
                a, b = mirror_ref[0, at], mirror_ref[1, at]
                parts.append((a * re + b * im, a * im - b * re))
            for t, (re, im) in enumerate(turn(parts, -1)):
                h_ref[t, 0, row] = re
                h_ref[t, 1, row] = im
            return carry

        lax.fori_loop(0, inner // 8, step16, 0)
        for t in range(RADIX):
            both = product(inv16_ref, (t,), jnp.concatenate([h_ref[t, 0], h_ref[t, 1]], 1))
            u_ref[:, 1, t] = (both[:inner, :lanes] - both[inner:, lanes:]).reshape(slivers, inner // slivers, lanes)


def split_table(values):
    high = lax.reduce_precision(values, 8, 7)
    return jnp.stack([high, values - high], -3).astype(jnp.bfloat16)


def make_tables(residues, inner, points, factor, transposed):
    shape = (RADIX, inner, inner)
    t = lax.broadcasted_iota(jnp.int32, shape, 0)
    time = t + RADIX * lax.broadcasted_iota(jnp.int32, shape, 1 if transposed else 2)
    step = 2 * SHARDS * lax.broadcasted_iota(jnp.int32, shape, 2 if transposed else 1)
    tables = []
    for residue in residues:
        phase = (time * (residue + step)) % points
        angle = phase.astype(jnp.float32) * (2.0 * math.pi / points)
        tables.append(split_table(jnp.concatenate([jnp.cos(angle) * factor, jnp.sin(angle) * factor], 1)))
    return jnp.stack(tables)


def on_device(grad_out, input_spectrum, filter_spectrum, skip_gain, interpret=False):
    column = lax.axis_index("tm")
    stream = lax.axis_index("dp")
    groups = lax.axis_size("dp")
    _, length, channels = grad_out.shape
    sliver = length // SHARDS
    inner = length // RADIX
    points = 2 * length * SHARDS
    factor = 1.0 / math.sqrt(points)
    params = functools.partial(pltpu.CompilerParams, vmem_limit_bytes=56 * 1024 * 1024)
    f32 = jnp.float32

    pick = (column >= 8).astype(jnp.int32)
    first = (column == 0).astype(jnp.int32)
    picks = jnp.stack([pick, first])

    mine = filter_spectrum[:, :, 0]
    part = length // groups
    give = lax.dynamic_index_in_dim(mine, (column < 8).astype(jnp.int32), 1, False)
    turned = lax.rev(lax.dynamic_slice_in_dim(give, (groups - 1 - stream) * part, part, 1), (1,))
    plain = lax.dynamic_slice_in_dim(give, stream * part, part, 1)
    sent = jnp.where(column == 8, plain, turned)
    swap = [(a, 15 - a) for a in range(8)] + [(8, 0)] + [(a, 16 - a) for a in range(9, 16)]
    mirror = lax.all_gather(lax.ppermute(sent, "tm", swap), "dp", axis=1, tiled=True)

    raw = lax.all_to_all(grad_out.reshape(SHARDS, sliver, channels), "tm", 0, 0, tiled=True)

    forward = make_tables([2 * column, 2 * column + 1], inner, points, factor, False)
    inverse = make_tables([2 * column + pick], inner, points, factor, True)[0]
    forward16 = make_tables([16], inner, points, factor, False)[0]
    inverse16 = make_tables([16], inner, points, factor, True)[0]

    rows = sliver // RADIX
    expanded = pl.pallas_call(
        expand_kernel,
        grid=(channels // LANES,),
        in_specs=[pl.BlockSpec((SHARDS, sliver, LANES), lambda c: (0, 0, c))],
        out_specs=pl.BlockSpec((SHARDS, 4, RADIX, rows, LANES), lambda c: (0, 0, 0, 0, c)),
        out_shape=jax.ShapeDtypeStruct((SHARDS, 4, RADIX, rows, channels), f32),
        compiler_params=params(),
        cost_estimate=pl.CostEstimate(flops=300 * length * channels // 16, bytes_accessed=5 * length * channels * 4, transcendentals=0),
        interpret=interpret,
        name="expand",
    )(raw)
    arrived = lax.all_to_all(expanded, "tm", 0, 0, tiled=True)

    def fixed(shape):
        return pl.BlockSpec(shape, lambda c, s: (0,) * len(shape), pipeline_mode=pl.Buffered(1))

    terms, inverted = pl.pallas_call(
        spectrum_kernel,
        grid_spec=pltpu.PrefetchScalarGridSpec(
            num_scalar_prefetch=1,
            grid=(channels // LANES,),
            in_specs=[
                pl.BlockSpec((SHARDS, 4, RADIX, rows, LANES), lambda c, s: (0, 0, 0, 0, c)),
                pl.BlockSpec((2, None, 2, None, length, LANES), lambda c, s: (0, 0, 0, 0, 0, c)),
                pl.BlockSpec((2, None, None, length, LANES), lambda c, s: (0, s[0], 0, 0, c)),
                pl.BlockSpec((2, length, LANES), lambda c, s: (0, 0, c)),
                fixed(forward.shape),
                fixed(inverse.shape),
                fixed(forward16.shape),
                fixed(inverse16.shape),
            ],
            out_specs=[
                pl.BlockSpec((2, 2, None, length, LANES), lambda c, s: (0, 0, 0, 0, c)),
                pl.BlockSpec((SHARDS, 2, RADIX, rows, LANES), lambda c, s: (0, 0, 0, 0, c)),
            ],
            scratch_shapes=[
                pltpu.VMEM((2, RADIX, 2, inner, LANES), f32),
                pltpu.VMEM((RADIX, 2, inner, LANES), f32),
            ],
        ),
        out_shape=[
            jax.ShapeDtypeStruct((2, 2, 1, length, channels), f32),
            jax.ShapeDtypeStruct((SHARDS, 2, RADIX, rows, channels), f32),
        ],
        compiler_params=params(),
        cost_estimate=pl.CostEstimate(flops=10**10, bytes_accessed=20 * length * channels * 4, transcendentals=0),
        interpret=interpret,
        name="spectrum",
    )(picks, arrived, input_spectrum, filter_spectrum, mirror, forward, inverse, forward16, inverse16)

    grad_filter = lax.psum_scatter(terms, "dp", scatter_dimension=3, tiled=True)
    landed = lax.all_to_all(inverted, "tm", 0, 0, tiled=True)
    combined = pl.pallas_call(
        combine_kernel,
        grid=(channels // LANES,),
        in_specs=[
            pl.BlockSpec((SHARDS, 2, RADIX, rows, LANES), lambda c: (0, 0, 0, 0, c)),
            pl.BlockSpec((SHARDS, sliver, LANES), lambda c: (0, 0, c)),
            pl.BlockSpec((1, LANES), lambda c: (0, c)),
        ],
        out_specs=pl.BlockSpec((SHARDS, sliver, LANES), lambda c: (0, 0, c)),
        out_shape=jax.ShapeDtypeStruct((SHARDS, sliver, channels), f32),
        compiler_params=params(),
        cost_estimate=pl.CostEstimate(flops=400 * length * channels // 16, bytes_accessed=4 * length * channels * 4, transcendentals=0),
        interpret=interpret,
        name="combine",
    )(landed, raw, skip_gain[None])
    back = lax.all_to_all(combined, "tm", 0, 0, tiled=True)
    return (back.reshape(1, length, channels), grad_filter)


def solution(mesh, interpret=False):
    return jax.shard_map(
        functools.partial(on_device, interpret=interpret),
        mesh=mesh,
        in_specs=(
            P("dp", "tm", None),
            P(None, "dp", None, "tm", None, None),
            P(None, None, "tm", None, None),
            P(),
        ),
        out_specs=(P("dp", "tm", None), P(None, None, "tm", "dp", None)),
        check_vma=False,
    )
```

```python
import functools
import math

import jax
import jax.numpy as jnp
import numpy as np
from jax import lax
from jax.experimental import pallas as pl
from jax.experimental.pallas import tpu as pltpu
from jax.sharding import PartitionSpec as P

LANES = 128
SHARDS = 16
RADIX = 4


def weighted(pairs):
    total = None
    for coefficient, value in pairs:
        if abs(coefficient) < 1e-12:
            continue
        if total is None:
            if abs(coefficient - 1.0) < 1e-12:
                total = value
            else:
                total = value * coefficient
        elif abs(coefficient - 1.0) < 1e-12:
            total = total + value
        elif abs(coefficient + 1.0) < 1e-12:
            total = total - value
        else:
            total = total + value * coefficient
    return total


def cos_at(numerator, denominator):
    return math.cos(2.0 * math.pi * (numerator % denominator) / denominator)


def sin_at(numerator, denominator):
    return math.sin(2.0 * math.pi * (numerator % denominator) / denominator)


def residues_of(x):
    total = {n: x[n] + x[16 - n] for n in range(1, 8)}
    diff = {n: x[n] - x[16 - n] for n in range(1, 8)}
    out = {}
    evens, odds = (2, 4, 6), (1, 3, 5, 7)
    for a in range(0, 5):
        even_re = weighted([(1.0, x[0]), (cos_at(8 * a, 16), x[8])] + [(cos_at(n * a, 16), total[n]) for n in evens])
        odd_re = weighted([(cos_at(n * a, 16), total[n]) for n in odds])
        even_im = weighted([(sin_at(n * a, 16), diff[n]) for n in evens])
        odd_im = weighted([(sin_at(n * a, 16), diff[n]) for n in odds])
        if a == 4:
            out[2 * a] = (even_re, -odd_im)
            continue
        re_low, re_high = even_re + odd_re, even_re - odd_re
        if a == 0:
            out[0], out[16] = (re_low, None), (re_high, None)
        else:
            out[2 * a] = (re_low, -(even_im + odd_im))
            out[16 - 2 * a] = (re_high, even_im - odd_im)
    for rho in (1, 3, 5, 7):
        even_re = weighted([(1.0, x[0])] + [(cos_at(n * rho, 32), diff[n]) for n in evens])
        odd_re = weighted([(cos_at(n * rho, 32), diff[n]) for n in odds])
        even_im = weighted([(sin_at(8 * rho, 32), x[8])] + [(sin_at(n * rho, 32), total[n]) for n in evens])
        odd_im = weighted([(sin_at(n * rho, 32), total[n]) for n in odds])
        out[rho] = (even_re + odd_re, -(even_im + odd_im))
        out[16 - rho] = (even_re - odd_re, even_im - odd_im)
    return out


def expand_kernel(x_ref, picked_ref, other_ref):
    groups = x_ref.shape[1] // RADIX // 8

    def step(index, carry):
        t, group = index // groups, index % groups
        row = pl.ds(pl.multiple_of(group * 8, 8), 8)
        values = [x_ref[n, pl.ds(group * 8 * RADIX + t, 8, stride=RADIX), :] for n in range(SHARDS)]
        found = residues_of(values)
        zero = jnp.zeros_like(values[0])
        for a in range(SHARDS):
            for rho in (2 * a, 2 * a + 1):
                if rho <= 16:
                    re, im = found[rho]
                    if rho == 0:
                        im = found[16][0]
                    elif rho == 16:
                        im = zero
                else:
                    re, im = found[32 - rho]
                    im = -im
                out_ref = picked_ref if (rho % 2 == 1) == (a >= 8) else other_ref
                out_ref[a, 0, t, row, :] = re
                out_ref[a, 1, t, row, :] = im
        return carry

    lax.fori_loop(0, RADIX * groups, step, 0)


def times_of(v0, v16, even, odd):
    out = [None] * 16
    ce, se, co, so = {}, {}, {}, {}
    for n in range(0, 5):
        c_even = weighted([(1.0, v0), (1.0 if n % 2 == 0 else -1.0, v16)] + [(cos_at(n * d, 16), even[d][0]) for d in (2, 4, 6)])
        c_odd = weighted([(cos_at(n * d, 16), even[d][0]) for d in (1, 3, 5, 7)])
        s_even = weighted([(sin_at(n * d, 16), even[d][1]) for d in (2, 4, 6)])
        s_odd = weighted([(sin_at(n * d, 16), even[d][1]) for d in (1, 3, 5, 7)])
        if n == 4:
            ce[4], se[4] = c_even, s_odd
        elif n == 0:
            ce[0], ce[8] = c_even + c_odd, c_even - c_odd
        else:
            ce[n], ce[8 - n] = c_even + c_odd, c_even - c_odd
            se[n], se[8 - n] = s_odd + s_even, s_odd - s_even
    re_sum = {q: odd[q][0] + odd[16 - q][0] for q in (1, 3, 5, 7)}
    re_diff = {q: odd[q][0] - odd[16 - q][0] for q in (1, 3, 5, 7)}
    im_sum = {q: odd[q][1] + odd[16 - q][1] for q in (1, 3, 5, 7)}
    im_diff = {q: odd[q][1] - odd[16 - q][1] for q in (1, 3, 5, 7)}
    for n in range(0, 9):
        re_of, im_of = (re_sum, im_diff) if n % 2 == 0 else (re_diff, im_sum)
        co[n] = weighted([(cos_at(n * q, 32), re_of[q]) for q in (1, 3, 5, 7)])
        so[n] = weighted([(sin_at(n * q, 32), im_of[q]) for q in (1, 3, 5, 7)])
    out[0] = ce[0] + co[0]
    out[8] = ce[8] + so[8]
    for n in range(1, 8):
        out[n] = (ce[n] - se[n]) + (co[n] + so[n])
        out[16 - n] = (ce[n] + se[n]) + (so[n] - co[n])
    return out


def combine_kernel(u_ref, out_ref):
    groups = out_ref.shape[1] // RADIX // 8

    def step(index, carry):
        t, group = index // groups, index % groups
        row = pl.ds(pl.multiple_of(group * 8, 8), 8)
        even = {d: (u_ref[d, 0, t, row, :], u_ref[d, 1, t, row, :]) for d in range(1, 8)}
        odd = {31 - 2 * d: (u_ref[d, 0, t, row, :], u_ref[d, 1, t, row, :]) for d in range(8, 16)}
        times = times_of(u_ref[0, 0, t, row, :], u_ref[0, 1, t, row, :], even, odd)
        rows = pl.ds(group * 8 * RADIX + t, 8, stride=RADIX)
        for n in range(SHARDS):
            out_ref[n, rows, :] = times[n]
        return carry

    lax.fori_loop(0, RADIX * groups, step, 0)


dot = functools.partial(jnp.dot, preferred_element_type=jnp.float32)


def halves_of(values):
    high = values.astype(jnp.bfloat16)
    low = (values - high.astype(jnp.float32)).astype(jnp.bfloat16)
    return high, low


def product(tables, t, values):
    high, low = halves_of(values)
    return [
        dot(tables[k][t], high) + (dot(tables[k][t], low) + dot(tables[k + 1][t], high)) for k in (0, 2)
    ]


def turn(parts, sign):
    (r0, i0), (r1, i1), (r2, i2), (r3, i3) = parts
    ar, ai, br, bi = r0 + r2, i0 + i2, r0 - r2, i0 - i2
    cr, ci, dr, di = r1 + r3, i1 + i3, r1 - r3, i1 - i3
    if sign < 0:
        dr, di = -dr, -di
    return (ar + cr, ai + ci), (br + di, bi - dr), (ar - cr, ai - ci), (br - di, bi + dr)


def forward_parts(z_ref, tables, s_ref, keep):
    inner, lanes = s_ref.shape[2:]
    for t in range(RADIX):
        re = z_ref[:, 0, t].reshape(inner, lanes)
        im = z_ref[:, 1, t].reshape(inner, lanes) * keep
        cosine, sine = product(tables, t, jnp.concatenate([re, im], 1))
        s_ref[t, 0] = cosine[:, :lanes] + sine[:, lanes:]
        s_ref[t, 1] = cosine[:, lanes:] - sine[:, :lanes]


def rows_at(index):
    return pl.ds(pl.multiple_of(index, 8), 8)


def write_terms(s_ref, row, at, saved_ref, term_ref, re, im):
    a, b = saved_ref[0, at], saved_ref[1, at]
    term_ref[0, at] = a * re + b * im
    term_ref[1, at] = a * im - b * re


def other_kernel(pick_ref, z_ref, *refs):
    tables = refs[:4]
    saved_ref, term_ref, s_ref = refs[4:]
    inner = s_ref.shape[2]
    forward_parts(z_ref, tables, s_ref, 1.0)

    def step(index, carry):
        row = rows_at(index * 8)
        parts = [(s_ref[t, 0, row], s_ref[t, 1, row]) for t in range(RADIX)]
        for q, (re, im) in enumerate(turn(parts, 1)):
            write_terms(s_ref, row, rows_at(q * inner + index * 8), saved_ref, term_ref, re, im)
        return carry

    lax.fori_loop(0, inner // 8, step, 0, unroll=2)


def spectrum_kernel(pick_ref, z_ref, *refs):
    tables, tables16, back, back16 = refs[0:4], refs[4:8], refs[8:12], refs[12:16]
    saved_ref, filt_ref, mirror_ref, term_ref, u_ref, s_ref = refs[16:]
    first = pick_ref[1]
    keep = (1 - first).astype(jnp.float32)
    inner, lanes = s_ref.shape[2:]
    slivers = u_ref.shape[0]

    def inverse_of(tables, slots):
        for t in range(RADIX):
            cosine, sine = product(tables, t, jnp.concatenate([s_ref[t, 0], s_ref[t, 1]], 1))
            values = (cosine[:, :lanes] - sine[:, lanes:], sine[:, :lanes] + cosine[:, lanes:])
            for slot, of in slots:
                u_ref[:, slot, t] = values[of].reshape(slivers, inner // slivers, lanes)

    forward_parts(z_ref, tables, s_ref, keep)

    def step(index, carry):
        row = rows_at(index * 8)
        parts = [(s_ref[t, 0, row], s_ref[t, 1, row]) for t in range(RADIX)]
        back_parts = []
        for q, (re, im) in enumerate(turn(parts, 1)):
            at = rows_at(q * inner + index * 8)
            write_terms(s_ref, row, at, saved_ref, term_ref, re, im)
            a = filt_ref[0, at] + keep * mirror_ref[0, at]
            b = keep * mirror_ref[1, at] - filt_ref[1, at]
            back_parts.append((a * re - b * im, a * im + b * re))
        for t, (re, im) in enumerate(turn(back_parts, -1)):
            s_ref[t, 0, row] = re
            s_ref[t, 1, row] = im
        return carry

    lax.fori_loop(0, inner // 8, step, 0, unroll=2)
    inverse_of(back, ((0, 0), (1, 1)))

    @pl.when(first == 1)
    def _():
        for t in range(RADIX):
            cosine, sine = product(tables16, t, z_ref[:, 1, t].reshape(inner, lanes))
            s_ref[t, 0] = cosine
            s_ref[t, 1] = -sine

        def step16(index, carry):
            row = rows_at(index * 8)
            parts = []
            for q, (re, im) in enumerate(turn([(s_ref[t, 0, row], s_ref[t, 1, row]) for t in range(RADIX)], 1)):
                at = rows_at(q * inner + index * 8)
                a, b = mirror_ref[0, at], mirror_ref[1, at]
                parts.append((a * re + b * im, a * im - b * re))
            for t, (re, im) in enumerate(turn(parts, -1)):
                s_ref[t, 0, row] = re
                s_ref[t, 1, row] = im
            return carry

        lax.fori_loop(0, inner // 8, step16, 0, unroll=2)
        inverse_of(back16, ((1, 0),))


def split_table(values):
    high = lax.reduce_precision(values, 8, 7)
    return [high.astype(jnp.bfloat16), (values - high).astype(jnp.bfloat16)]


def base_table(inner, points, transposed):
    time = np.arange(RADIX)[:, None, None] + RADIX * np.arange(inner)[None, None, :]
    angle = 2.0 * np.pi * ((time * 2 * SHARDS * np.arange(inner)[None, :, None]) % points) / points
    if transposed:
        angle = angle.transpose(0, 2, 1)
    return np.cos(angle).astype(np.float32), np.sin(angle).astype(np.float32)


def make_table(residue, inner, points, factor, transposed):
    base_cos, base_sin = base_table(inner, points, transposed)
    time = jnp.arange(RADIX)[:, None] + RADIX * jnp.arange(inner)[None, :]
    angle = ((time * residue) % points).astype(jnp.float32) * (2.0 * math.pi / points)
    twist_cos, twist_sin = lax.optimization_barrier((jnp.cos(angle) * factor, jnp.sin(angle) * factor))
    at = (slice(None), slice(None), None) if transposed else (slice(None), None, slice(None))
    twist_cos, twist_sin = twist_cos[at], twist_sin[at]
    cosine = base_cos * twist_cos - base_sin * twist_sin
    sine = base_sin * twist_cos + base_cos * twist_sin
    return split_table(cosine) + split_table(sine)


def fixed_table(residue, inner, points, factor, transposed):
    time = np.arange(RADIX)[:, None, None] + RADIX * np.arange(inner)[None, None, :]
    phase = (time * (residue + 2 * SHARDS * np.arange(inner))[None, :, None]) % points
    if transposed:
        phase = phase.transpose(0, 2, 1)
    found = []
    for values in (np.cos(2.0 * np.pi * phase / points) * factor, np.sin(2.0 * np.pi * phase / points) * factor):
        high = values.astype(np.float32).astype(jnp.bfloat16)
        found += [high, (values - high.astype(np.float64)).astype(jnp.bfloat16)]
    return found


def on_device(grad_out, input_spectrum, filter_spectrum, skip_gain, interpret=False):
    column = lax.axis_index("tm")
    stream = lax.axis_index("dp")
    groups = lax.axis_size("dp")
    _, length, channels = grad_out.shape
    sliver = length // SHARDS
    inner = length // RADIX
    points = 2 * length * SHARDS
    factor = 1.0 / math.sqrt(points)
    params = functools.partial(pltpu.CompilerParams, vmem_limit_bytes=56 * 1024 * 1024)
    f32 = jnp.float32

    pick = (column >= 8).astype(jnp.int32)
    first = (column == 0).astype(jnp.int32)
    picks = jnp.stack([pick, first])

    rows = sliver // RADIX
    raw = lax.all_to_all(grad_out.reshape(SHARDS, sliver, channels), "tm", 0, 0, tiled=True)

    part = length // groups
    filt = filter_spectrum[:, :, 0]
    give = lax.dynamic_index_in_dim(filt, (column < 8).astype(jnp.int32), 1, False)
    turned = lax.rev(lax.dynamic_slice_in_dim(give, (groups - 1 - stream) * part, part, 1), (1,))
    plain = lax.dynamic_slice_in_dim(give, stream * part, part, 1)
    sent = jnp.where(column == 8, plain, turned)
    swap = [(a, 15 - a) for a in range(8)] + [(8, 0)] + [(a, 16 - a) for a in range(9, 16)]
    swapped, raw = lax.optimization_barrier((lax.ppermute(sent, "tm", swap), raw))
    mirror = lax.all_gather(swapped, "dp", axis=1, tiled=True)

    z_shape = (SHARDS, 2, RADIX, rows)
    z_block = pl.BlockSpec(z_shape + (LANES,), lambda c: (0, 0, 0, 0, c))
    picked, other = pl.pallas_call(
        expand_kernel,
        grid=(channels // LANES,),
        in_specs=[pl.BlockSpec((SHARDS, sliver, LANES), lambda c: (0, 0, c))],
        out_specs=[z_block, z_block],
        out_shape=[jax.ShapeDtypeStruct(z_shape + (channels,), f32)] * 2,
        compiler_params=params(),
        cost_estimate=pl.CostEstimate(flops=300 * length * channels // 16, bytes_accessed=5 * length * channels * 4, transcendentals=0),
        interpret=interpret,
        name="expand",
    )(raw)
    z_picked = lax.all_to_all(picked, "tm", 0, 0, tiled=True)
    z_picked, other = lax.optimization_barrier((z_picked, other))
    z_other = lax.all_to_all(other, "tm", 0, 0, tiled=True)

    table = functools.partial(make_table, inner=inner, points=points, factor=factor)
    known = functools.partial(fixed_table, residue=16, inner=inner, points=points, factor=factor)
    residue = 2 * column + pick
    picked_tables = table(residue, transposed=False) + known(transposed=False)
    picked_tables += table(residue, transposed=True) + known(transposed=True)
    other_tables = table(2 * column + 1 - pick, transposed=False)

    def fixed(values):
        return pl.BlockSpec(values.shape, lambda c, s: (0,) * values.ndim, pipeline_mode=pl.Buffered(1))

    z_spec = pl.BlockSpec(z_shape + (LANES,), lambda c, s: (0, 0, 0, 0, c))
    saved_shape = (2, None, None, None, length, LANES)
    term_shape = jax.ShapeDtypeStruct((2, length, channels), f32)
    term_spec = pl.BlockSpec((2, length, LANES), lambda c, s: (0, 0, c))
    scratch = [pltpu.VMEM((RADIX, 2, inner, LANES), f32)]

    terms, inverted = pl.pallas_call(
        spectrum_kernel,
        grid_spec=pltpu.PrefetchScalarGridSpec(
            num_scalar_prefetch=1,
            grid=(channels // LANES,),
            in_specs=[z_spec]
            + [fixed(table) for table in picked_tables]
            + [
                pl.BlockSpec(saved_shape, lambda c, s: (0, 0, s[0], 0, 0, c)),
                pl.BlockSpec((2, None, None, length, LANES), lambda c, s: (0, s[0], 0, 0, c)),
                pl.BlockSpec((2, length, LANES), lambda c, s: (0, 0, c)),
            ],
            out_specs=[
                term_spec,
                z_spec,
            ],
            scratch_shapes=scratch,
        ),
        out_shape=[term_shape, jax.ShapeDtypeStruct((SHARDS, 2, RADIX, rows, channels), f32)],
        compiler_params=params(),
        cost_estimate=pl.CostEstimate(flops=10**10, bytes_accessed=12 * length * channels * 4, transcendentals=0),
        interpret=interpret,
        name="spectrum",
    )(picks, z_picked, *picked_tables, input_spectrum, filter_spectrum, mirror)
    terms, inverted, z_other = lax.optimization_barrier((terms, inverted, z_other))
    other_terms = pl.pallas_call(
        other_kernel,
        grid_spec=pltpu.PrefetchScalarGridSpec(
            num_scalar_prefetch=1,
            grid=(channels // LANES,),
            in_specs=[z_spec]
            + [fixed(table) for table in other_tables]
            + [
                pl.BlockSpec(saved_shape, lambda c, s: (0, 0, 1 - s[0], 0, 0, c)),
            ],
            out_specs=term_spec,
            scratch_shapes=scratch,
        ),
        out_shape=term_shape,
        compiler_params=params(),
        cost_estimate=pl.CostEstimate(flops=7 * 10**9, bytes_accessed=8 * length * channels * 4, transcendentals=0),
        interpret=interpret,
        name="other",
    )(picks, z_other, *other_tables, input_spectrum)

    landed = lax.all_to_all(inverted, "tm", 0, 0, tiled=True)
    ours = lax.psum_scatter(terms, "dp", scatter_dimension=1, tiled=True)
    other_terms, _ = lax.optimization_barrier((other_terms, landed))
    others = lax.psum_scatter(other_terms, "dp", scatter_dimension=1, tiled=True)
    combined = pl.pallas_call(
        combine_kernel,
        grid=(channels // LANES,),
        in_specs=[
            pl.BlockSpec((SHARDS, 2, RADIX, rows, LANES), lambda c: (0, 0, 0, 0, c)),
        ],
        out_specs=pl.BlockSpec((SHARDS, sliver, LANES), lambda c: (0, 0, c)),
        out_shape=jax.ShapeDtypeStruct((SHARDS, sliver, channels), f32),
        compiler_params=params(),
        cost_estimate=pl.CostEstimate(flops=400 * length * channels // 16, bytes_accessed=4 * length * channels * 4, transcendentals=0),
        interpret=interpret,
        name="combine",
    )(landed)
    back = lax.all_to_all(combined, "tm", 0, 0, tiled=True)
    grad_filter = jnp.where(pick == 0, jnp.stack([ours, others], 1), jnp.stack([others, ours], 1))[:, :, None]
    return (back.reshape(1, length, channels) + skip_gain * grad_out, grad_filter)


def solution(mesh, interpret=False):
    return jax.shard_map(
        functools.partial(on_device, interpret=interpret),
        mesh=mesh,
        in_specs=(
            P("dp", "tm", None),
            P(None, "dp", None, "tm", None, None),
            P(None, None, "tm", None, None),
            P(),
        ),
        out_specs=(P("dp", "tm", None), P(None, None, "tm", "dp", None)),
        check_vma=False,
    )
```

```python
import functools
import math

import jax
import jax.numpy as jnp
import numpy as np
from jax import lax
from jax.experimental import pallas as pl
from jax.experimental.pallas import tpu as pltpu
from jax.sharding import PartitionSpec as P

LANES = 128
SHARDS = 16
RADIX = 4


def weighted(pairs):
    total = None
    for coefficient, value in pairs:
        if abs(coefficient) < 1e-12:
            continue
        if total is None:
            if abs(coefficient - 1.0) < 1e-12:
                total = value
            else:
                total = value * coefficient
        elif abs(coefficient - 1.0) < 1e-12:
            total = total + value
        elif abs(coefficient + 1.0) < 1e-12:
            total = total - value
        else:
            total = total + value * coefficient
    return total


def cos_at(numerator, denominator):
    return math.cos(2.0 * math.pi * (numerator % denominator) / denominator)


def sin_at(numerator, denominator):
    return math.sin(2.0 * math.pi * (numerator % denominator) / denominator)


def residues_of(x):
    total = {n: x[n] + x[16 - n] for n in range(1, 8)}
    diff = {n: x[n] - x[16 - n] for n in range(1, 8)}
    out = {}
    evens, odds = (2, 4, 6), (1, 3, 5, 7)
    for a in range(0, 5):
        even_re = weighted([(1.0, x[0]), (cos_at(8 * a, 16), x[8])] + [(cos_at(n * a, 16), total[n]) for n in evens])
        odd_re = weighted([(cos_at(n * a, 16), total[n]) for n in odds])
        even_im = weighted([(sin_at(n * a, 16), diff[n]) for n in evens])
        odd_im = weighted([(sin_at(n * a, 16), diff[n]) for n in odds])
        if a == 4:
            out[2 * a] = (even_re, -odd_im)
            continue
        re_low, re_high = even_re + odd_re, even_re - odd_re
        if a == 0:
            out[0], out[16] = (re_low, None), (re_high, None)
        else:
            out[2 * a] = (re_low, -(even_im + odd_im))
            out[16 - 2 * a] = (re_high, even_im - odd_im)
    for rho in (1, 3, 5, 7):
        even_re = weighted([(1.0, x[0])] + [(cos_at(n * rho, 32), diff[n]) for n in evens])
        odd_re = weighted([(cos_at(n * rho, 32), diff[n]) for n in odds])
        even_im = weighted([(sin_at(8 * rho, 32), x[8])] + [(sin_at(n * rho, 32), total[n]) for n in evens])
        odd_im = weighted([(sin_at(n * rho, 32), total[n]) for n in odds])
        out[rho] = (even_re + odd_re, -(even_im + odd_im))
        out[16 - rho] = (even_re - odd_re, even_im - odd_im)
    return out


def expand_block(x_ref, out_ref, other):
    groups = x_ref.shape[1] // RADIX // 8

    def step(index, carry):
        t, group = index // groups, index % groups
        row = pl.ds(pl.multiple_of(group * 8, 8), 8)
        values = [x_ref[n, pl.ds(group * 8 * RADIX + t, 8, stride=RADIX), :] for n in range(SHARDS)]
        found = residues_of(values)
        zero = jnp.zeros_like(values[0])
        for a in range(SHARDS):
            rho = 2 * a + ((a >= 8) != other)
            if rho <= 16:
                re, im = found[rho]
                if rho == 0:
                    im = found[16][0]
                elif rho == 16:
                    im = zero
            else:
                re, im = found[32 - rho]
                im = -im
            out_ref[a, 0, t, row, :] = re
            out_ref[a, 1, t, row, :] = im
        return carry

    lax.fori_loop(0, RADIX * groups, step, 0)


def expand_kernel(blocks, x_ref, out_ref):
    @pl.when(pl.program_id(0) < blocks)
    def _():
        expand_block(x_ref, out_ref, False)

    @pl.when(pl.program_id(0) >= blocks)
    def _():
        expand_block(x_ref, out_ref, True)


def times_of(v0, v16, even, odd):
    out = [None] * 16
    ce, se, co, so = {}, {}, {}, {}
    for n in range(0, 5):
        c_even = weighted([(1.0, v0), (1.0 if n % 2 == 0 else -1.0, v16)] + [(cos_at(n * d, 16), even[d][0]) for d in (2, 4, 6)])
        c_odd = weighted([(cos_at(n * d, 16), even[d][0]) for d in (1, 3, 5, 7)])
        s_even = weighted([(sin_at(n * d, 16), even[d][1]) for d in (2, 4, 6)])
        s_odd = weighted([(sin_at(n * d, 16), even[d][1]) for d in (1, 3, 5, 7)])
        if n == 4:
            ce[4], se[4] = c_even, s_odd
        elif n == 0:
            ce[0], ce[8] = c_even + c_odd, c_even - c_odd
        else:
            ce[n], ce[8 - n] = c_even + c_odd, c_even - c_odd
            se[n], se[8 - n] = s_odd + s_even, s_odd - s_even
    re_sum = {q: odd[q][0] + odd[16 - q][0] for q in (1, 3, 5, 7)}
    re_diff = {q: odd[q][0] - odd[16 - q][0] for q in (1, 3, 5, 7)}
    im_sum = {q: odd[q][1] + odd[16 - q][1] for q in (1, 3, 5, 7)}
    im_diff = {q: odd[q][1] - odd[16 - q][1] for q in (1, 3, 5, 7)}
    for n in range(0, 9):
        re_of, im_of = (re_sum, im_diff) if n % 2 == 0 else (re_diff, im_sum)
        co[n] = weighted([(cos_at(n * q, 32), re_of[q]) for q in (1, 3, 5, 7)])
        so[n] = weighted([(sin_at(n * q, 32), im_of[q]) for q in (1, 3, 5, 7)])
    out[0] = ce[0] + co[0]
    out[8] = ce[8] + so[8]
    for n in range(1, 8):
        out[n] = (ce[n] - se[n]) + (co[n] + so[n])
        out[16 - n] = (ce[n] + se[n]) + (so[n] - co[n])
    return out


def combine_kernel(u_ref, x_ref, gain_ref, out_ref):
    groups = out_ref.shape[1] // RADIX // 8

    def step(index, carry):
        t, group = index // groups, index % groups
        row = pl.ds(pl.multiple_of(group * 8, 8), 8)
        even = {d: (u_ref[d, 0, t, row, :], u_ref[d, 1, t, row, :]) for d in range(1, 8)}
        odd = {31 - 2 * d: (u_ref[d, 0, t, row, :], u_ref[d, 1, t, row, :]) for d in range(8, 16)}
        times = times_of(u_ref[0, 0, t, row, :], u_ref[0, 1, t, row, :], even, odd)
        rows = pl.ds(group * 8 * RADIX + t, 8, stride=RADIX)
        gain = gain_ref[0:1, :]
        for n in range(SHARDS):
            out_ref[n, rows, :] = times[n] + gain * x_ref[n, rows, :]
        return carry

    lax.fori_loop(0, RADIX * groups, step, 0)


dot = functools.partial(jnp.dot, preferred_element_type=jnp.float32)


def halves_of(values):
    high = values.astype(jnp.bfloat16)
    low = (values - high.astype(jnp.float32)).astype(jnp.bfloat16)
    return high, low


def product(tables, t, values):
    high, low = halves_of(values)
    return [
        dot(tables[k][t], high) + (dot(tables[k][t], low) + dot(tables[k + 1][t], high)) for k in (0, 2)
    ]


def turn(parts, sign):
    (r0, i0), (r1, i1), (r2, i2), (r3, i3) = parts
    ar, ai, br, bi = r0 + r2, i0 + i2, r0 - r2, i0 - i2
    cr, ci, dr, di = r1 + r3, i1 + i3, r1 - r3, i1 - i3
    if sign < 0:
        dr, di = -dr, -di
    return (ar + cr, ai + ci), (br + di, bi - dr), (ar - cr, ai - ci), (br - di, bi + dr)


def forward_parts(z_ref, tables, s_ref, keep):
    inner, lanes = s_ref.shape[2:]
    for t in range(RADIX):
        re = z_ref[:, 0, t].reshape(inner, lanes)
        im = z_ref[:, 1, t].reshape(inner, lanes) * keep
        cosine, sine = product(tables, t, jnp.concatenate([re, im], 1))
        s_ref[t, 0] = cosine[:, :lanes] + sine[:, lanes:]
        s_ref[t, 1] = cosine[:, lanes:] - sine[:, :lanes]


def rows_at(index):
    return pl.ds(pl.multiple_of(index, 8), 8)


def write_terms(s_ref, row, at, saved_ref, term_ref, re, im):
    a, b = saved_ref[0, at], saved_ref[1, at]
    term_ref[0, at] = a * re + b * im
    term_ref[1, at] = a * im - b * re


def other_kernel(pick_ref, z_ref, *refs):
    tables = refs[:4]
    saved_ref, _, term_ref, s_ref = refs[4:]
    inner = s_ref.shape[2]
    forward_parts(z_ref, tables, s_ref, 1.0)

    def step(index, carry):
        row = rows_at(index * 8)
        parts = [(s_ref[t, 0, row], s_ref[t, 1, row]) for t in range(RADIX)]
        for q, (re, im) in enumerate(turn(parts, 1)):
            write_terms(s_ref, row, rows_at(q * inner + index * 8), saved_ref, term_ref, re, im)
        return carry

    lax.fori_loop(0, inner // 8, step, 0, unroll=2)


def spectrum_kernel(pick_ref, z_ref, *refs):
    tables, tables16, back, back16 = refs[0:4], refs[4:8], refs[8:12], refs[12:16]
    saved_ref, filt_ref, mirror_ref, term_ref, u_ref, s_ref = refs[16:]
    first = pick_ref[1]
    keep = (1 - first).astype(jnp.float32)
    inner, lanes = s_ref.shape[2:]
    slivers = u_ref.shape[0]

    def inverse_of(tables, slots):
        for t in range(RADIX):
            cosine, sine = product(tables, t, jnp.concatenate([s_ref[t, 0], s_ref[t, 1]], 1))
            values = (cosine[:, :lanes] - sine[:, lanes:], sine[:, :lanes] + cosine[:, lanes:])
            for slot, of in slots:
                u_ref[:, slot, t] = values[of].reshape(slivers, inner // slivers, lanes)

    forward_parts(z_ref, tables, s_ref, keep)

    def step(index, carry):
        row = rows_at(index * 8)
        parts = [(s_ref[t, 0, row], s_ref[t, 1, row]) for t in range(RADIX)]
        back_parts = []
        for q, (re, im) in enumerate(turn(parts, 1)):
            at = rows_at(q * inner + index * 8)
            write_terms(s_ref, row, at, saved_ref, term_ref, re, im)
            a = filt_ref[0, at] + keep * mirror_ref[0, at]
            b = keep * mirror_ref[1, at] - filt_ref[1, at]
            back_parts.append((a * re - b * im, a * im + b * re))
        for t, (re, im) in enumerate(turn(back_parts, -1)):
            s_ref[t, 0, row] = re
            s_ref[t, 1, row] = im
        return carry

    lax.fori_loop(0, inner // 8, step, 0, unroll=2)
    inverse_of(back, ((0, 0), (1, 1)))

    @pl.when(first == 1)
    def _():
        for t in range(RADIX):
            cosine, sine = product(tables16, t, z_ref[:, 1, t].reshape(inner, lanes))
            s_ref[t, 0] = cosine
            s_ref[t, 1] = -sine

        def step16(index, carry):
            row = rows_at(index * 8)
            parts = []
            for q, (re, im) in enumerate(turn([(s_ref[t, 0, row], s_ref[t, 1, row]) for t in range(RADIX)], 1)):
                at = rows_at(q * inner + index * 8)
                a, b = mirror_ref[0, at], mirror_ref[1, at]
                parts.append((a * re + b * im, a * im - b * re))
            for t, (re, im) in enumerate(turn(parts, -1)):
                s_ref[t, 0, row] = re
                s_ref[t, 1, row] = im
            return carry

        lax.fori_loop(0, inner // 8, step16, 0, unroll=2)
        inverse_of(back16, ((1, 0),))


def split_table(values):
    high = lax.reduce_precision(values, 8, 7)
    return [high.astype(jnp.bfloat16), (values - high).astype(jnp.bfloat16)]


def base_table(inner, points, transposed):
    time = np.arange(RADIX)[:, None, None] + RADIX * np.arange(inner)[None, None, :]
    angle = 2.0 * np.pi * ((time * 2 * SHARDS * np.arange(inner)[None, :, None]) % points) / points
    if transposed:
        angle = angle.transpose(0, 2, 1)
    return np.cos(angle).astype(np.float32), np.sin(angle).astype(np.float32)


def make_table(residue, inner, points, factor, transposed):
    base_cos, base_sin = base_table(inner, points, transposed)
    time = jnp.arange(RADIX)[:, None] + RADIX * jnp.arange(inner)[None, :]
    angle = ((time * residue) % points).astype(jnp.float32) * (2.0 * math.pi / points)
    twist_cos, twist_sin = lax.optimization_barrier((jnp.cos(angle) * factor, jnp.sin(angle) * factor))
    at = (slice(None), slice(None), None) if transposed else (slice(None), None, slice(None))
    twist_cos, twist_sin = twist_cos[at], twist_sin[at]
    cosine = base_cos * twist_cos - base_sin * twist_sin
    sine = base_sin * twist_cos + base_cos * twist_sin
    return split_table(cosine) + split_table(sine)


def fixed_table(residue, inner, points, factor, transposed):
    time = np.arange(RADIX)[:, None, None] + RADIX * np.arange(inner)[None, None, :]
    phase = (time * (residue + 2 * SHARDS * np.arange(inner))[None, :, None]) % points
    if transposed:
        phase = phase.transpose(0, 2, 1)
    found = []
    for values in (np.cos(2.0 * np.pi * phase / points) * factor, np.sin(2.0 * np.pi * phase / points) * factor):
        high = values.astype(np.float32).astype(jnp.bfloat16)
        found += [high, (values - high.astype(np.float64)).astype(jnp.bfloat16)]
    return found


def on_device(grad_out, input_spectrum, filter_spectrum, skip_gain, interpret=False):
    column = lax.axis_index("tm")
    stream = lax.axis_index("dp")
    groups = lax.axis_size("dp")
    _, length, channels = grad_out.shape
    sliver = length // SHARDS
    inner = length // RADIX
    points = 2 * length * SHARDS
    factor = 1.0 / math.sqrt(points)
    params = functools.partial(pltpu.CompilerParams, vmem_limit_bytes=56 * 1024 * 1024)
    f32 = jnp.float32

    pick = (column >= 8).astype(jnp.int32)
    first = (column == 0).astype(jnp.int32)
    picks = jnp.stack([pick, first])

    rows = sliver // RADIX
    blocks = channels // LANES
    early = blocks // 2
    raw = lax.all_to_all(grad_out.reshape(SHARDS, sliver, channels), "tm", 0, 0, tiled=True)

    part = length // groups
    filt = filter_spectrum[:, :, 0]
    give = lax.dynamic_index_in_dim(filt, (column < 8).astype(jnp.int32), 1, False)
    turned = lax.rev(lax.dynamic_slice_in_dim(give, (groups - 1 - stream) * part, part, 1), (1,))
    plain = lax.dynamic_slice_in_dim(give, stream * part, part, 1)
    sent = jnp.where(column == 8, plain, turned)
    table = functools.partial(make_table, inner=inner, points=points, factor=factor)
    known = functools.partial(fixed_table, residue=16, inner=inner, points=points, factor=factor)
    residue = 2 * column + pick
    made = [table(residue, transposed=False), table(residue, transposed=True), table(2 * column + 1 - pick, transposed=False)]
    raw, sent, made = lax.optimization_barrier((raw, sent, made))
    picked_tables = made[0] + known(transposed=False) + made[1] + known(transposed=True)
    other_tables = made[2]
    swap = [(a, 15 - a) for a in range(8)] + [(8, 0)] + [(a, 16 - a) for a in range(9, 16)]
    swapped = lax.ppermute(sent, "tm", swap)

    z_shape = (SHARDS, 2, RADIX, rows)

    def expand(picked, first_other, others, name):
        return pl.pallas_call(
            functools.partial(expand_kernel, picked),
            grid=(picked + others,),
            in_specs=[
                pl.BlockSpec((SHARDS, sliver, LANES), lambda c: (0, 0, jnp.where(c < picked, c, c - picked + first_other)))
            ],
            out_specs=pl.BlockSpec(z_shape + (LANES,), lambda c: (0, 0, 0, 0, c)),
            out_shape=jax.ShapeDtypeStruct(z_shape + ((picked + others) * LANES,), f32),
            compiler_params=params(),
            cost_estimate=pl.CostEstimate(
                flops=300 * sliver * LANES * (picked + others), bytes_accessed=(picked + others) * 2**21, transcendentals=0
            ),
            interpret=interpret,
            name=name,
        )(raw)

    first_part = expand(blocks, 0, early, "expand")
    rest = expand(0, early, blocks - early, "expand_rest")
    swapped, first_part, rest = lax.optimization_barrier((swapped, first_part, rest))
    mirror = lax.all_gather(swapped, "dp", axis=1, tiled=True)
    z_first = lax.all_to_all(first_part, "tm", 0, 0, tiled=True)
    z_first, rest = lax.optimization_barrier((z_first, rest))
    z_rest = lax.all_to_all(rest, "tm", 0, 0, tiled=True)

    def fixed(values):
        return pl.BlockSpec(values.shape, lambda c, s: (0,) * values.ndim, pipeline_mode=pl.Buffered(1))

    def z_spec(shift):
        return pl.BlockSpec(z_shape + (LANES,), lambda c, s: (0, 0, 0, 0, c + shift))

    saved_shape = (2, None, None, None, length, LANES)
    term_shape = jax.ShapeDtypeStruct((2, 2, 1, length, channels), f32)
    term_block = (2, None, None, length, LANES)
    scratch = [pltpu.VMEM((RADIX, 2, inner, LANES), f32)]

    terms, inverted = pl.pallas_call(
        spectrum_kernel,
        grid_spec=pltpu.PrefetchScalarGridSpec(
            num_scalar_prefetch=1,
            grid=(channels // LANES,),
            in_specs=[z_spec(0)]
            + [fixed(table) for table in picked_tables]
            + [
                pl.BlockSpec(saved_shape, lambda c, s: (0, 0, s[0], 0, 0, c)),
                pl.BlockSpec((2, None, None, length, LANES), lambda c, s: (0, s[0], 0, 0, c)),
                pl.BlockSpec((2, length, LANES), lambda c, s: (0, 0, c)),
            ],
            out_specs=[
                pl.BlockSpec(term_block, lambda c, s: (0, s[0], 0, 0, c)),
                pl.BlockSpec(z_shape + (LANES,), lambda c, s: (0, 0, 0, 0, c)),
            ],
            scratch_shapes=scratch,
        ),
        out_shape=[term_shape, jax.ShapeDtypeStruct((SHARDS, 2, RADIX, rows, channels), f32)],
        compiler_params=params(),
        cost_estimate=pl.CostEstimate(flops=10**10, bytes_accessed=12 * length * channels * 4, transcendentals=0),
        interpret=interpret,
        name="spectrum",
    )(picks, z_first, *picked_tables, input_spectrum, filter_spectrum, mirror)

    def second(z, at, first_block, count, terms, name):
        return pl.pallas_call(
            other_kernel,
            grid_spec=pltpu.PrefetchScalarGridSpec(
                num_scalar_prefetch=1,
                grid=(count,),
                in_specs=[z_spec(at)]
                + [fixed(table) for table in other_tables]
                + [
                    pl.BlockSpec(saved_shape, lambda c, s: (0, 0, 1 - s[0], 0, 0, c + first_block)),
                    pl.BlockSpec(memory_space=pl.ANY),
                ],
                out_specs=pl.BlockSpec(term_block, lambda c, s: (0, 1 - s[0], 0, 0, c + first_block)),
                scratch_shapes=scratch,
            ),
            out_shape=term_shape,
            input_output_aliases={2 + len(other_tables) + 1: 0},
            compiler_params=params(),
            cost_estimate=pl.CostEstimate(
                flops=2 * 10**9 * count, bytes_accessed=count * 2 * length * LANES * 4 * 3, transcendentals=0
            ),
            interpret=interpret,
            name=name,
        )(picks, z, *other_tables, input_spectrum, terms)

    terms = second(z_first, blocks, 0, early, terms, "other")
    terms, inverted, z_rest = lax.optimization_barrier((terms, inverted, z_rest))
    terms = second(z_rest, 0, early, blocks - early, terms, "other_rest")
    terms, inverted = lax.optimization_barrier((terms, inverted))
    grad_filter = lax.psum_scatter(terms, "dp", scatter_dimension=3, tiled=True)
    landed = lax.all_to_all(inverted, "tm", 0, 0, tiled=True)
    combined = pl.pallas_call(
        combine_kernel,
        grid=(channels // LANES,),
        in_specs=[
            pl.BlockSpec((SHARDS, 2, RADIX, rows, LANES), lambda c: (0, 0, 0, 0, c)),
            pl.BlockSpec((SHARDS, sliver, LANES), lambda c: (0, 0, c)),
            pl.BlockSpec((1, LANES), lambda c: (0, c)),
        ],
        out_specs=pl.BlockSpec((SHARDS, sliver, LANES), lambda c: (0, 0, c)),
        out_shape=jax.ShapeDtypeStruct((SHARDS, sliver, channels), f32),
        compiler_params=params(),
        cost_estimate=pl.CostEstimate(flops=400 * length * channels // 16, bytes_accessed=4 * length * channels * 4, transcendentals=0),
        interpret=interpret,
        name="combine",
    )(landed, raw, skip_gain[None])
    back = lax.all_to_all(combined, "tm", 0, 0, tiled=True)
    return (back.reshape(1, length, channels), grad_filter)


def solution(mesh, interpret=False):
    return jax.shard_map(
        functools.partial(on_device, interpret=interpret),
        mesh=mesh,
        in_specs=(
            P("dp", "tm", None),
            P(None, "dp", None, "tm", None, None),
            P(None, None, "tm", None, None),
            P(),
        ),
        out_specs=(P("dp", "tm", None), P(None, None, "tm", "dp", None)),
        check_vma=False,
    )
```

```python
import functools
import math

import jax
import jax.numpy as jnp
import numpy as np
from jax import lax
from jax.experimental import pallas as pl
from jax.experimental.pallas import tpu as pltpu
from jax.sharding import PartitionSpec as P

LANES = 128
SHARDS = 16
RADIX = 4


def weighted(pairs):
    total = None
    for coefficient, value in pairs:
        if abs(coefficient) < 1e-12:
            continue
        if total is None:
            if abs(coefficient - 1.0) < 1e-12:
                total = value
            else:
                total = value * coefficient
        elif abs(coefficient - 1.0) < 1e-12:
            total = total + value
        elif abs(coefficient + 1.0) < 1e-12:
            total = total - value
        else:
            total = total + value * coefficient
    return total


def cos_at(numerator, denominator):
    return math.cos(2.0 * math.pi * (numerator % denominator) / denominator)


def sin_at(numerator, denominator):
    return math.sin(2.0 * math.pi * (numerator % denominator) / denominator)


def residues_of(x):
    total = {n: x[n] + x[16 - n] for n in range(1, 8)}
    diff = {n: x[n] - x[16 - n] for n in range(1, 8)}
    out = {}
    evens, odds = (2, 4, 6), (1, 3, 5, 7)
    for a in range(0, 5):
        even_re = weighted([(1.0, x[0]), (cos_at(8 * a, 16), x[8])] + [(cos_at(n * a, 16), total[n]) for n in evens])
        odd_re = weighted([(cos_at(n * a, 16), total[n]) for n in odds])
        even_im = weighted([(sin_at(n * a, 16), diff[n]) for n in evens])
        odd_im = weighted([(sin_at(n * a, 16), diff[n]) for n in odds])
        if a == 4:
            out[2 * a] = (even_re, -odd_im)
            continue
        re_low, re_high = even_re + odd_re, even_re - odd_re
        if a == 0:
            out[0], out[16] = (re_low, None), (re_high, None)
        else:
            out[2 * a] = (re_low, -(even_im + odd_im))
            out[16 - 2 * a] = (re_high, even_im - odd_im)
    for rho in (1, 3, 5, 7):
        even_re = weighted([(1.0, x[0])] + [(cos_at(n * rho, 32), diff[n]) for n in evens])
        odd_re = weighted([(cos_at(n * rho, 32), diff[n]) for n in odds])
        even_im = weighted([(sin_at(8 * rho, 32), x[8])] + [(sin_at(n * rho, 32), total[n]) for n in evens])
        odd_im = weighted([(sin_at(n * rho, 32), total[n]) for n in odds])
        out[rho] = (even_re + odd_re, -(even_im + odd_im))
        out[16 - rho] = (even_re - odd_re, even_im - odd_im)
    return out


def expand_block(x_ref, out_ref, other):
    groups = x_ref.shape[1] // RADIX // 8

    def step(index, carry):
        t, group = index // groups, index % groups
        row = pl.ds(pl.multiple_of(group * 8, 8), 8)
        values = [x_ref[n, pl.ds(group * 8 * RADIX + t, 8, stride=RADIX), :] for n in range(SHARDS)]
        found = residues_of(values)
        zero = jnp.zeros_like(values[0])
        for a in range(SHARDS):
            rho = 2 * a + ((a >= 8) != other)
            if rho <= 16:
                re, im = found[rho]
                if rho == 0:
                    im = found[16][0]
                elif rho == 16:
                    im = zero
            else:
                re, im = found[32 - rho]
                im = -im
            out_ref[a, 0, t, row, :] = re
            out_ref[a, 1, t, row, :] = im
        return carry

    lax.fori_loop(0, RADIX * groups, step, 0, unroll=True)


def expand_kernel(blocks, x_ref, out_ref):
    @pl.when(pl.program_id(0) < blocks)
    def _():
        expand_block(x_ref, out_ref, False)

    @pl.when(pl.program_id(0) >= blocks)
    def _():
        expand_block(x_ref, out_ref, True)


def times_of(v0, v16, even, odd):
    out = [None] * 16
    ce, se, co, so = {}, {}, {}, {}
    for n in range(0, 5):
        c_even = weighted([(1.0, v0), (1.0 if n % 2 == 0 else -1.0, v16)] + [(cos_at(n * d, 16), even[d][0]) for d in (2, 4, 6)])
        c_odd = weighted([(cos_at(n * d, 16), even[d][0]) for d in (1, 3, 5, 7)])
        s_even = weighted([(sin_at(n * d, 16), even[d][1]) for d in (2, 4, 6)])
        s_odd = weighted([(sin_at(n * d, 16), even[d][1]) for d in (1, 3, 5, 7)])
        if n == 4:
            ce[4], se[4] = c_even, s_odd
        elif n == 0:
            ce[0], ce[8] = c_even + c_odd, c_even - c_odd
        else:
            ce[n], ce[8 - n] = c_even + c_odd, c_even - c_odd
            se[n], se[8 - n] = s_odd + s_even, s_odd - s_even
    re_sum = {q: odd[q][0] + odd[16 - q][0] for q in (1, 3, 5, 7)}
    re_diff = {q: odd[q][0] - odd[16 - q][0] for q in (1, 3, 5, 7)}
    im_sum = {q: odd[q][1] + odd[16 - q][1] for q in (1, 3, 5, 7)}
    im_diff = {q: odd[q][1] - odd[16 - q][1] for q in (1, 3, 5, 7)}
    for n in range(0, 9):
        re_of, im_of = (re_sum, im_diff) if n % 2 == 0 else (re_diff, im_sum)
        co[n] = weighted([(cos_at(n * q, 32), re_of[q]) for q in (1, 3, 5, 7)])
        so[n] = weighted([(sin_at(n * q, 32), im_of[q]) for q in (1, 3, 5, 7)])
    out[0] = ce[0] + co[0]
    out[8] = ce[8] + so[8]
    for n in range(1, 8):
        out[n] = (ce[n] - se[n]) + (co[n] + so[n])
        out[16 - n] = (ce[n] + se[n]) + (so[n] - co[n])
    return out


def combine_kernel(u_ref, x_ref, gain_ref, out_ref):
    groups = out_ref.shape[1] // RADIX // 8

    def step(index, carry):
        t, group = index // groups, index % groups
        row = pl.ds(pl.multiple_of(group * 8, 8), 8)
        even = {d: (u_ref[d, 0, t, row, :], u_ref[d, 1, t, row, :]) for d in range(1, 8)}
        odd = {31 - 2 * d: (u_ref[d, 0, t, row, :], u_ref[d, 1, t, row, :]) for d in range(8, 16)}
        times = times_of(u_ref[0, 0, t, row, :], u_ref[0, 1, t, row, :], even, odd)
        rows = pl.ds(group * 8 * RADIX + t, 8, stride=RADIX)
        gain = gain_ref[0:1, :]
        for n in range(SHARDS):
            out_ref[n, rows, :] = times[n] + gain * x_ref[n, rows, :]
        return carry

    lax.fori_loop(0, RADIX * groups, step, 0, unroll=True)


dot = functools.partial(jnp.dot, preferred_element_type=jnp.float32)


def halves_of(values):
    high = values.astype(jnp.bfloat16)
    low = (values - high.astype(jnp.float32)).astype(jnp.bfloat16)
    return high, low


def product(tables, t, values):
    high, low = halves_of(values)
    return [
        dot(tables[k][t], high) + (dot(tables[k][t], low) + dot(tables[k + 1][t], high)) for k in (0, 2)
    ]


def turn(parts, sign):
    (r0, i0), (r1, i1), (r2, i2), (r3, i3) = parts
    ar, ai, br, bi = r0 + r2, i0 + i2, r0 - r2, i0 - i2
    cr, ci, dr, di = r1 + r3, i1 + i3, r1 - r3, i1 - i3
    if sign < 0:
        dr, di = -dr, -di
    return (ar + cr, ai + ci), (br + di, bi - dr), (ar - cr, ai - ci), (br - di, bi + dr)


def forward_parts(z_ref, blocks, tables, s_ref, keep):
    inner, lanes = s_ref.shape[2:]
    for t in range(RADIX):
        re = [z_ref[:, c, 0, t].reshape(inner, LANES) for c in blocks]
        im = [z_ref[:, c, 1, t].reshape(inner, LANES) * keep for c in blocks]
        cosine, sine = product(tables, t, jnp.concatenate(re + im, 1))
        s_ref[t, 0] = cosine[:, :lanes] + sine[:, lanes:]
        s_ref[t, 1] = cosine[:, lanes:] - sine[:, :lanes]


def rows_at(index):
    return pl.ds(pl.multiple_of(index, 8), 8)


def write_terms(s_ref, row, at, saved_ref, term_ref, re, im):
    a, b = saved_ref[0, at], saved_ref[1, at]
    term_ref[0, at] = a * re + b * im
    term_ref[1, at] = a * im - b * re


def other_kernel(pick_ref, z_ref, *refs):
    tables = refs[:4]
    saved_ref, _, term_ref, s_ref = refs[4:]
    inner = s_ref.shape[2]
    forward_parts(z_ref, [0], tables, s_ref, 1.0)

    def step(index, carry):
        row = rows_at(index * 8)
        parts = [(s_ref[t, 0, row], s_ref[t, 1, row]) for t in range(RADIX)]
        for q, (re, im) in enumerate(turn(parts, 1)):
            write_terms(s_ref, row, rows_at(q * inner + index * 8), saved_ref, term_ref, re, im)
        return carry

    lax.fori_loop(0, inner // 8, step, 0, unroll=2)


def spectrum_kernel(pick_ref, z_ref, *refs):
    tables, tables16, back, back16 = refs[0:4], refs[4:8], refs[8:12], refs[12:16]
    saved_ref, filt_ref, mirror_ref, term_ref, u_ref, s_ref = refs[16:]
    first = pick_ref[1]
    keep = (1 - first).astype(jnp.float32)
    inner, lanes = s_ref.shape[2:]
    slivers, blocks = u_ref.shape[:2]

    def inverse_of(tables, slots):
        for t in range(RADIX):
            cosine, sine = product(tables, t, jnp.concatenate([s_ref[t, 0], s_ref[t, 1]], 1))
            values = (cosine[:, :lanes] - sine[:, lanes:], sine[:, :lanes] + cosine[:, lanes:])
            for slot, of in slots:
                for c in range(blocks):
                    u_ref[:, c, slot, t] = values[of][:, c * LANES : (c + 1) * LANES].reshape(slivers, inner // slivers, LANES)

    forward_parts(z_ref, range(blocks), tables, s_ref, keep)

    def step(index, carry):
        row = rows_at(index * 8)
        parts = [(s_ref[t, 0, row], s_ref[t, 1, row]) for t in range(RADIX)]
        back_parts = []
        for q, (re, im) in enumerate(turn(parts, 1)):
            at = rows_at(q * inner + index * 8)
            write_terms(s_ref, row, at, saved_ref, term_ref, re, im)
            a = filt_ref[0, at] + keep * mirror_ref[0, at]
            b = keep * mirror_ref[1, at] - filt_ref[1, at]
            back_parts.append((a * re - b * im, a * im + b * re))
        for t, (re, im) in enumerate(turn(back_parts, -1)):
            s_ref[t, 0, row] = re
            s_ref[t, 1, row] = im
        return carry

    lax.fori_loop(0, inner // 8, step, 0, unroll=2)
    inverse_of(back, ((0, 0), (1, 1)))

    @pl.when(first == 1)
    def _():
        for t in range(RADIX):
            values = jnp.concatenate([z_ref[:, c, 1, t].reshape(inner, LANES) for c in range(blocks)], 1)
            cosine, sine = product(tables16, t, values)
            s_ref[t, 0] = cosine
            s_ref[t, 1] = -sine

        def step16(index, carry):
            row = rows_at(index * 8)
            parts = []
            for q, (re, im) in enumerate(turn([(s_ref[t, 0, row], s_ref[t, 1, row]) for t in range(RADIX)], 1)):
                at = rows_at(q * inner + index * 8)
                a, b = mirror_ref[0, at], mirror_ref[1, at]
                parts.append((a * re + b * im, a * im - b * re))
            for t, (re, im) in enumerate(turn(parts, -1)):
                s_ref[t, 0, row] = re
                s_ref[t, 1, row] = im
            return carry

        lax.fori_loop(0, inner // 8, step16, 0, unroll=2)
        inverse_of(back16, ((1, 0),))


def split_table(values):
    high = lax.reduce_precision(values, 8, 7)
    return [high.astype(jnp.bfloat16), (values - high).astype(jnp.bfloat16)]


def base_table(inner, points, transposed):
    time = np.arange(RADIX)[:, None, None] + RADIX * np.arange(inner)[None, None, :]
    angle = 2.0 * np.pi * ((time * 2 * SHARDS * np.arange(inner)[None, :, None]) % points) / points
    if transposed:
        angle = angle.transpose(0, 2, 1)
    return np.cos(angle).astype(np.float32), np.sin(angle).astype(np.float32)


def make_table(residue, inner, points, factor, transposed):
    base_cos, base_sin = base_table(inner, points, transposed)
    time = np.arange(RADIX, dtype=np.int32)[:, None] + RADIX * np.arange(inner, dtype=np.int32)[None, :]
    angle = ((time * residue) % points).astype(jnp.float32) * (2.0 * math.pi / points)
    twist_cos, twist_sin = lax.optimization_barrier((jnp.cos(angle) * factor, jnp.sin(angle) * factor))
    at = (slice(None), slice(None), None) if transposed else (slice(None), None, slice(None))
    twist_cos, twist_sin = twist_cos[at], twist_sin[at]
    cosine = base_cos * twist_cos - base_sin * twist_sin
    sine = base_sin * twist_cos + base_cos * twist_sin
    return split_table(cosine) + split_table(sine)


def fixed_table(residue, inner, points, factor, transposed):
    time = np.arange(RADIX)[:, None, None] + RADIX * np.arange(inner)[None, None, :]
    phase = (time * (residue + 2 * SHARDS * np.arange(inner))[None, :, None]) % points
    if transposed:
        phase = phase.transpose(0, 2, 1)
    found = []
    for values in (np.cos(2.0 * np.pi * phase / points) * factor, np.sin(2.0 * np.pi * phase / points) * factor):
        high = values.astype(np.float32).astype(jnp.bfloat16)
        found += [high, (values - high.astype(np.float64)).astype(jnp.bfloat16)]
    return found


def on_device(grad_out, input_spectrum, filter_spectrum, skip_gain, interpret=False):
    column = lax.axis_index("tm")
    stream = lax.axis_index("dp")
    groups = lax.axis_size("dp")
    _, length, channels = grad_out.shape
    sliver = length // SHARDS
    inner = length // RADIX
    points = 2 * length * SHARDS
    factor = 1.0 / math.sqrt(points)
    params = functools.partial(pltpu.CompilerParams, vmem_limit_bytes=56 * 1024 * 1024)
    f32 = jnp.float32

    pick = (column >= 8).astype(jnp.int32)
    first = (column == 0).astype(jnp.int32)
    picks = jnp.stack([pick, first])

    rows = sliver // RADIX
    blocks = channels // LANES
    early = blocks // 2

    part = length // groups
    filt = filter_spectrum[:, :, 0]
    give = lax.dynamic_index_in_dim(filt, (column < 8).astype(jnp.int32), 1, False)
    turned = lax.rev(lax.dynamic_slice_in_dim(give, (groups - 1 - stream) * part, part, 1), (1,))
    plain = lax.dynamic_slice_in_dim(give, stream * part, part, 1)
    sent = jnp.where(column == 8, plain, turned)
    grad_out, sent, picks, pick = lax.optimization_barrier((grad_out, sent, picks, pick))
    raw = lax.all_to_all(grad_out.reshape(SHARDS, sliver, channels), "tm", 0, 0, tiled=True)
    raw, sent = lax.optimization_barrier((raw, sent))
    swap = [(a, 15 - a) for a in range(8)] + [(8, 0)] + [(a, 16 - a) for a in range(9, 16)]
    swapped = lax.ppermute(sent, "tm", swap)

    late, _ = lax.optimization_barrier((column, raw))
    table = functools.partial(make_table, inner=inner, points=points, factor=factor)
    known = functools.partial(fixed_table, residue=16, inner=inner, points=points, factor=factor)
    residue = 2 * late + pick
    made = [table(residue, transposed=False), table(residue, transposed=True), table(2 * late + 1 - pick, transposed=False)]
    raw, made = lax.optimization_barrier((raw, made))
    picked_tables = made[0] + known(transposed=False) + made[1] + known(transposed=True)
    other_tables = made[2]

    z_tail = (2, RADIX, rows, LANES)

    def expand(raw, picked, first_other, others, name):
        return pl.pallas_call(
            functools.partial(expand_kernel, picked),
            grid=(picked + others,),
            in_specs=[
                pl.BlockSpec((SHARDS, sliver, LANES), lambda c: (0, 0, jnp.where(c < picked, c, c - picked + first_other)))
            ],
            out_specs=pl.BlockSpec((SHARDS, None) + z_tail, lambda c: (0, c, 0, 0, 0, 0)),
            out_shape=jax.ShapeDtypeStruct((SHARDS, picked + others) + z_tail, f32),
            compiler_params=params(),
            cost_estimate=pl.CostEstimate(flops=2**20, bytes_accessed=2**20, transcendentals=0),
            interpret=interpret,
            name=name,
        )(raw)

    first_part = expand(raw, blocks, 0, early, "expand")
    swapped, first_part, raw = lax.optimization_barrier((swapped, first_part, raw))
    rest = expand(raw, 0, early, blocks - early, "expand_rest")
    swapped, first_part, rest = lax.optimization_barrier((swapped, first_part, rest))
    mirror = lax.all_gather(swapped, "dp", axis=1, tiled=True)
    z_first = lax.all_to_all(first_part, "tm", 0, 0, tiled=True)
    z_first, rest = lax.optimization_barrier((z_first, rest))
    z_rest = lax.all_to_all(rest, "tm", 0, 0, tiled=True)

    def fixed(values):
        return pl.BlockSpec(values.shape, lambda c, s: (0,) * values.ndim, pipeline_mode=pl.Buffered(1))

    def z_spec(shift):
        return pl.BlockSpec((SHARDS, 1) + z_tail, lambda c, s: (0, c + shift, 0, 0, 0, 0))

    saved_shape = (2, None, None, None, length, LANES)
    term_shape = jax.ShapeDtypeStruct((2, 2, 1, length, channels), f32)
    term_block = (2, None, None, length, LANES)
    scratch = [pltpu.VMEM((RADIX, 2, inner, LANES), f32)]

    wide = min(2 * LANES, channels)
    terms, inverted = pl.pallas_call(
        spectrum_kernel,
        grid_spec=pltpu.PrefetchScalarGridSpec(
            num_scalar_prefetch=1,
            grid=(channels // wide,),
            in_specs=[pl.BlockSpec((SHARDS, wide // LANES) + z_tail, lambda c, s: (0, c, 0, 0, 0, 0))]
            + [fixed(table) for table in picked_tables]
            + [
                pl.BlockSpec(saved_shape[:-1] + (wide,), lambda c, s: (0, 0, s[0], 0, 0, c)),
                pl.BlockSpec((2, None, None, length, wide), lambda c, s: (0, s[0], 0, 0, c)),
                pl.BlockSpec((2, length, wide), lambda c, s: (0, 0, c)),
            ],
            out_specs=[
                pl.BlockSpec(term_block[:-1] + (wide,), lambda c, s: (0, s[0], 0, 0, c)),
                pl.BlockSpec((SHARDS, wide // LANES) + z_tail, lambda c, s: (0, c, 0, 0, 0, 0)),
            ],
            scratch_shapes=[pltpu.VMEM((RADIX, 2, inner, wide), f32)],
        ),
        out_shape=[term_shape, jax.ShapeDtypeStruct((SHARDS, blocks) + z_tail, f32)],
        compiler_params=params(),
        cost_estimate=pl.CostEstimate(flops=10**10, bytes_accessed=12 * length * channels * 4, transcendentals=0),
        interpret=interpret,
        name="spectrum",
    )(picks, z_first, *picked_tables, input_spectrum, filter_spectrum, mirror)

    def second(z, at, first_block, count, terms, name):
        return pl.pallas_call(
            other_kernel,
            grid_spec=pltpu.PrefetchScalarGridSpec(
                num_scalar_prefetch=1,
                grid=(count,),
                in_specs=[z_spec(at)]
                + [fixed(table) for table in other_tables]
                + [
                    pl.BlockSpec(saved_shape, lambda c, s: (0, 0, 1 - s[0], 0, 0, c + first_block)),
                    pl.BlockSpec(memory_space=pl.ANY),
                ],
                out_specs=pl.BlockSpec(term_block, lambda c, s: (0, 1 - s[0], 0, 0, c + first_block)),
                scratch_shapes=scratch,
            ),
            out_shape=term_shape,
            input_output_aliases={2 + len(other_tables) + 1: 0},
            compiler_params=params(),
            cost_estimate=pl.CostEstimate(
                flops=2 * 10**9 * count, bytes_accessed=count * 2 * length * LANES * 4 * 3, transcendentals=0
            ),
            interpret=interpret,
            name=name,
        )(picks, z, *other_tables, input_spectrum, terms)

    terms = second(z_first, blocks, 0, early, terms, "other")
    terms, inverted, z_rest = lax.optimization_barrier((terms, inverted, z_rest))
    terms = second(z_rest, 0, early, blocks - early, terms, "other_rest")
    terms, inverted = lax.optimization_barrier((terms, inverted))
    grad_filter = lax.psum_scatter(terms, "dp", scatter_dimension=3, tiled=True)
    landed = lax.all_to_all(inverted, "tm", 0, 0, tiled=True)
    combined = pl.pallas_call(
        combine_kernel,
        grid=(channels // LANES,),
        in_specs=[
            pl.BlockSpec((SHARDS, None) + z_tail, lambda c: (0, c, 0, 0, 0, 0)),
            pl.BlockSpec((SHARDS, sliver, LANES), lambda c: (0, 0, c)),
            pl.BlockSpec((1, LANES), lambda c: (0, c)),
        ],
        out_specs=pl.BlockSpec((SHARDS, sliver, LANES), lambda c: (0, 0, c)),
        out_shape=jax.ShapeDtypeStruct((SHARDS, sliver, channels), f32),
        compiler_params=params(),
        cost_estimate=pl.CostEstimate(flops=400 * length * channels // 16, bytes_accessed=4 * length * channels * 4, transcendentals=0),
        interpret=interpret,
        name="combine",
    )(landed, raw, skip_gain[None])
    back = lax.all_to_all(combined, "tm", 0, 0, tiled=True)
    return (back.reshape(1, length, channels), grad_filter)


def solution(mesh, interpret=False):
    return jax.shard_map(
        functools.partial(on_device, interpret=interpret),
        mesh=mesh,
        in_specs=(
            P("dp", "tm", None),
            P(None, "dp", None, "tm", None, None),
            P(None, None, "tm", None, None),
            P(),
        ),
        out_specs=(P("dp", "tm", None), P(None, None, "tm", "dp", None)),
        check_vma=False,
    )
```

```python
import functools
import math

import jax
import jax.numpy as jnp
import numpy as np
from jax import lax
from jax.experimental import pallas as pl
from jax.experimental.pallas import tpu as pltpu
from jax.sharding import PartitionSpec as P

LANES = 128
SHARDS = 16
RADIX = 4


def weighted(pairs):
    total = None
    for coefficient, value in pairs:
        if abs(coefficient) < 1e-12:
            continue
        if total is None:
            if abs(coefficient - 1.0) < 1e-12:
                total = value
            else:
                total = value * coefficient
        elif abs(coefficient - 1.0) < 1e-12:
            total = total + value
        elif abs(coefficient + 1.0) < 1e-12:
            total = total - value
        else:
            total = total + value * coefficient
    return total


def cos_at(numerator, denominator):
    return math.cos(2.0 * math.pi * (numerator % denominator) / denominator)


def sin_at(numerator, denominator):
    return math.sin(2.0 * math.pi * (numerator % denominator) / denominator)


def residues_of(x):
    total = {n: x[n] + x[16 - n] for n in range(1, 8)}
    diff = {n: x[n] - x[16 - n] for n in range(1, 8)}
    out = {}
    evens, odds = (2, 4, 6), (1, 3, 5, 7)
    for a in range(0, 5):
        even_re = weighted([(1.0, x[0]), (cos_at(8 * a, 16), x[8])] + [(cos_at(n * a, 16), total[n]) for n in evens])
        odd_re = weighted([(cos_at(n * a, 16), total[n]) for n in odds])
        even_im = weighted([(sin_at(n * a, 16), diff[n]) for n in evens])
        odd_im = weighted([(sin_at(n * a, 16), diff[n]) for n in odds])
        if a == 4:
            out[2 * a] = (even_re, -odd_im)
            continue
        re_low, re_high = even_re + odd_re, even_re - odd_re
        if a == 0:
            out[0], out[16] = (re_low, None), (re_high, None)
        else:
            out[2 * a] = (re_low, -(even_im + odd_im))
            out[16 - 2 * a] = (re_high, even_im - odd_im)
    for rho in (1, 3, 5, 7):
        even_re = weighted([(1.0, x[0])] + [(cos_at(n * rho, 32), diff[n]) for n in evens])
        odd_re = weighted([(cos_at(n * rho, 32), diff[n]) for n in odds])
        even_im = weighted([(sin_at(8 * rho, 32), x[8])] + [(sin_at(n * rho, 32), total[n]) for n in evens])
        odd_im = weighted([(sin_at(n * rho, 32), total[n]) for n in odds])
        out[rho] = (even_re + odd_re, -(even_im + odd_im))
        out[16 - rho] = (even_re - odd_re, even_im - odd_im)
    return out


def expand_block(x_ref, out_ref, other):
    groups = x_ref.shape[1] // RADIX // 8

    def step(index, carry):
        t, group = index // groups, index % groups
        row = pl.ds(pl.multiple_of(group * 8, 8), 8)
        values = [x_ref[n, pl.ds(group * 8 * RADIX + t, 8, stride=RADIX), :] for n in range(SHARDS)]
        found = residues_of(values)
        zero = jnp.zeros_like(values[0])
        for a in range(SHARDS):
            rho = 2 * a + ((a >= 8) != other)
            if rho <= 16:
                re, im = found[rho]
                if rho == 0:
                    im = found[16][0]
                elif rho == 16:
                    im = zero
            else:
                re, im = found[32 - rho]
                im = -im
            out_ref[a, 0, t, row, :] = re
            out_ref[a, 1, t, row, :] = im
        return carry

    lax.fori_loop(0, RADIX * groups, step, 0, unroll=True)


def expand_kernel(blocks, x_ref, out_ref):
    @pl.when(pl.program_id(0) < blocks)
    def _():
        expand_block(x_ref, out_ref, False)

    @pl.when(pl.program_id(0) >= blocks)
    def _():
        expand_block(x_ref, out_ref, True)


def times_of(v0, v16, even, odd):
    out = [None] * 16
    ce, se, co, so = {}, {}, {}, {}
    for n in range(0, 5):
        c_even = weighted([(1.0, v0), (1.0 if n % 2 == 0 else -1.0, v16)] + [(cos_at(n * d, 16), even[d][0]) for d in (2, 4, 6)])
        c_odd = weighted([(cos_at(n * d, 16), even[d][0]) for d in (1, 3, 5, 7)])
        s_even = weighted([(sin_at(n * d, 16), even[d][1]) for d in (2, 4, 6)])
        s_odd = weighted([(sin_at(n * d, 16), even[d][1]) for d in (1, 3, 5, 7)])
        if n == 4:
            ce[4], se[4] = c_even, s_odd
        elif n == 0:
            ce[0], ce[8] = c_even + c_odd, c_even - c_odd
        else:
            ce[n], ce[8 - n] = c_even + c_odd, c_even - c_odd
            se[n], se[8 - n] = s_odd + s_even, s_odd - s_even
    re_sum = {q: odd[q][0] + odd[16 - q][0] for q in (1, 3, 5, 7)}
    re_diff = {q: odd[q][0] - odd[16 - q][0] for q in (1, 3, 5, 7)}
    im_sum = {q: odd[q][1] + odd[16 - q][1] for q in (1, 3, 5, 7)}
    im_diff = {q: odd[q][1] - odd[16 - q][1] for q in (1, 3, 5, 7)}
    for n in range(0, 9):
        re_of, im_of = (re_sum, im_diff) if n % 2 == 0 else (re_diff, im_sum)
        co[n] = weighted([(cos_at(n * q, 32), re_of[q]) for q in (1, 3, 5, 7)])
        so[n] = weighted([(sin_at(n * q, 32), im_of[q]) for q in (1, 3, 5, 7)])
    out[0] = ce[0] + co[0]
    out[8] = ce[8] + so[8]
    for n in range(1, 8):
        out[n] = (ce[n] - se[n]) + (co[n] + so[n])
        out[16 - n] = (ce[n] + se[n]) + (so[n] - co[n])
    return out


def combine_kernel(u_ref, x_ref, gain_ref, out_ref):
    groups = out_ref.shape[1] // RADIX // 8

    def step(index, carry):
        t, group = index // groups, index % groups
        row = pl.ds(pl.multiple_of(group * 8, 8), 8)
        even = {d: (u_ref[d, 0, t, row, :], u_ref[d, 1, t, row, :]) for d in range(1, 8)}
        odd = {31 - 2 * d: (u_ref[d, 0, t, row, :], u_ref[d, 1, t, row, :]) for d in range(8, 16)}
        times = times_of(u_ref[0, 0, t, row, :], u_ref[0, 1, t, row, :], even, odd)
        rows = pl.ds(group * 8 * RADIX + t, 8, stride=RADIX)
        gain = gain_ref[0:1, :]
        for n in range(SHARDS):
            out_ref[n, rows, :] = times[n] + gain * x_ref[n, rows, :]
        return carry

    lax.fori_loop(0, RADIX * groups, step, 0, unroll=True)


dot = functools.partial(jnp.dot, preferred_element_type=jnp.float32)


def halves_of(values):
    high = values.astype(jnp.bfloat16)
    low = (values - high.astype(jnp.float32)).astype(jnp.bfloat16)
    return high, low


def product(tables, t, values):
    high, low = halves_of(values)
    return [
        dot(tables[k][t], high) + (dot(tables[k][t], low) + dot(tables[k + 1][t], high)) for k in (0, 2)
    ]


def turn(parts, sign):
    (r0, i0), (r1, i1), (r2, i2), (r3, i3) = parts
    ar, ai, br, bi = r0 + r2, i0 + i2, r0 - r2, i0 - i2
    cr, ci, dr, di = r1 + r3, i1 + i3, r1 - r3, i1 - i3
    if sign < 0:
        dr, di = -dr, -di
    return (ar + cr, ai + ci), (br + di, bi - dr), (ar - cr, ai - ci), (br - di, bi + dr)


def forward_parts(z_ref, blocks, tables, s_ref):
    inner, lanes = s_ref.shape[2:]
    for t in range(RADIX):
        re = [z_ref[:, c, 0, t].reshape(inner, LANES) for c in blocks]
        im = [z_ref[:, c, 1, t].reshape(inner, LANES) for c in blocks]
        cosine, sine = product(tables, t, jnp.concatenate(re + im, 1))
        s_ref[t, 0] = cosine[:, :lanes] + sine[:, lanes:]
        s_ref[t, 1] = cosine[:, lanes:] - sine[:, :lanes]


def forward_real(z_ref, slot, blocks, tables, s_ref):
    inner = s_ref.shape[2]
    for t in range(RADIX):
        values = jnp.concatenate([z_ref[:, c, slot, t].reshape(inner, LANES) for c in blocks], 1)
        cosine, sine = product(tables, t, values)
        s_ref[t, 0] = cosine
        s_ref[t, 1] = -sine


def rows_at(index):
    return pl.ds(pl.multiple_of(index, 8), 8)


def write_terms(s_ref, row, at, saved_ref, term_ref, re, im):
    a, b = saved_ref[0, at], saved_ref[1, at]
    term_ref[0, at] = a * re + b * im
    term_ref[1, at] = a * im - b * re


def other_kernel(pick_ref, z_ref, *refs):
    tables = refs[:4]
    saved_ref, _, term_ref, s_ref = refs[4:]
    inner = s_ref.shape[2]
    forward_parts(z_ref, [0], tables, s_ref)

    def step(index, carry):
        row = rows_at(index * 8)
        parts = [(s_ref[t, 0, row], s_ref[t, 1, row]) for t in range(RADIX)]
        for q, (re, im) in enumerate(turn(parts, 1)):
            write_terms(s_ref, row, rows_at(q * inner + index * 8), saved_ref, term_ref, re, im)
        return carry

    lax.fori_loop(0, inner // 8, step, 0, unroll=2)


def spectrum_kernel(pick_ref, z_ref, *refs):
    tables, tables16, back, back16 = refs[0:4], refs[4:8], refs[8:12], refs[12:16]
    saved_ref, filt_ref, mirror_ref, term_ref, u_ref, s_ref = refs[16:]
    first = pick_ref[1]
    inner, lanes = s_ref.shape[2:]
    slivers, blocks = u_ref.shape[:2]

    def put(values, slot, t):
        for c in range(blocks):
            u_ref[:, c, slot, t] = values[:, c * LANES : (c + 1) * LANES].reshape(slivers, inner // slivers, LANES)

    def inverse_real(tables, slot):
        for t in range(RADIX):
            total = None
            for k, part in ((0, s_ref[t, 0]), (2, -s_ref[t, 1])):
                high, low = halves_of(part)
                found = dot(tables[k][t], high) + (dot(tables[k][t], low) + dot(tables[k + 1][t], high))
                total = found if total is None else total + found
            put(total, slot, t)

    def middle(weigh, with_terms):
        def step(index, carry):
            row = rows_at(index * 8)
            parts = [(s_ref[t, 0, row], s_ref[t, 1, row]) for t in range(RADIX)]
            back_parts = []
            for q, (re, im) in enumerate(turn(parts, 1)):
                at = rows_at(q * inner + index * 8)
                if with_terms:
                    write_terms(s_ref, row, at, saved_ref, term_ref, re, im)
                a, b = weigh(at)
                back_parts.append((a * re - b * im, a * im + b * re))
            for t, (re, im) in enumerate(turn(back_parts, -1)):
                s_ref[t, 0, row] = re
                s_ref[t, 1, row] = im
            return carry

        lax.fori_loop(0, inner // 8, step, 0, unroll=2)

    @pl.when(first == 0)
    def _():
        forward_parts(z_ref, range(blocks), tables, s_ref)
        middle(lambda at: (filt_ref[0, at] + mirror_ref[0, at], mirror_ref[1, at] - filt_ref[1, at]), True)
        for t in range(RADIX):
            cosine, sine = product(back, t, jnp.concatenate([s_ref[t, 0], s_ref[t, 1]], 1))
            put(cosine[:, :lanes] - sine[:, lanes:], 0, t)
            put(sine[:, :lanes] + cosine[:, lanes:], 1, t)

    @pl.when(first == 1)
    def _():
        forward_real(z_ref, 0, range(blocks), tables, s_ref)
        middle(lambda at: (filt_ref[0, at], -filt_ref[1, at]), True)
        inverse_real(back, 0)
        forward_real(z_ref, 1, range(blocks), tables16, s_ref)
        middle(lambda at: (mirror_ref[0, at], mirror_ref[1, at]), False)
        inverse_real(back16, 1)


def split_table(values):
    high = lax.reduce_precision(values, 8, 7)
    return [high.astype(jnp.bfloat16), (values - high).astype(jnp.bfloat16)]


def base_table(inner, points, transposed):
    time = np.arange(RADIX)[:, None, None] + RADIX * np.arange(inner)[None, None, :]
    angle = 2.0 * np.pi * ((time * 2 * SHARDS * np.arange(inner)[None, :, None]) % points) / points
    if transposed:
        angle = angle.transpose(0, 2, 1)
    return np.cos(angle).astype(np.float32), np.sin(angle).astype(np.float32)


def make_table(residue, inner, points, factor, transposed):
    base_cos, base_sin = base_table(inner, points, transposed)
    time = np.arange(RADIX, dtype=np.int32)[:, None] + RADIX * np.arange(inner, dtype=np.int32)[None, :]
    angle = ((time * residue) % points).astype(jnp.float32) * (2.0 * math.pi / points)
    twist_cos, twist_sin = lax.optimization_barrier((jnp.cos(angle) * factor, jnp.sin(angle) * factor))
    at = (slice(None), slice(None), None) if transposed else (slice(None), None, slice(None))
    twist_cos, twist_sin = twist_cos[at], twist_sin[at]
    cosine = base_cos * twist_cos - base_sin * twist_sin
    sine = base_sin * twist_cos + base_cos * twist_sin
    return split_table(cosine) + split_table(sine)


def fixed_table(residue, inner, points, factor, transposed):
    time = np.arange(RADIX)[:, None, None] + RADIX * np.arange(inner)[None, None, :]
    phase = (time * (residue + 2 * SHARDS * np.arange(inner))[None, :, None]) % points
    if transposed:
        phase = phase.transpose(0, 2, 1)
    found = []
    for values in (np.cos(2.0 * np.pi * phase / points) * factor, np.sin(2.0 * np.pi * phase / points) * factor):
        high = values.astype(np.float32).astype(jnp.bfloat16)
        found += [high, (values - high.astype(np.float64)).astype(jnp.bfloat16)]
    return found


def on_device(grad_out, input_spectrum, filter_spectrum, skip_gain, interpret=False):
    column = lax.axis_index("tm")
    stream = lax.axis_index("dp")
    groups = lax.axis_size("dp")
    _, length, channels = grad_out.shape
    sliver = length // SHARDS
    inner = length // RADIX
    points = 2 * length * SHARDS
    factor = 1.0 / math.sqrt(points)
    params = functools.partial(pltpu.CompilerParams, vmem_limit_bytes=56 * 1024 * 1024)
    f32 = jnp.float32

    pick = (column >= 8).astype(jnp.int32)
    first = (column == 0).astype(jnp.int32)
    picks = jnp.stack([pick, first])

    rows = sliver // RADIX
    blocks = channels // LANES
    early = blocks // 2

    part = length // groups
    filt = filter_spectrum[:, :, 0]
    give = lax.dynamic_index_in_dim(filt, (column < 8).astype(jnp.int32), 1, False)
    sent = lax.rev(lax.dynamic_slice_in_dim(give, (groups - 1 - stream) * part, part, 1), (1,))
    grad_out, sent, picks, pick = lax.optimization_barrier((grad_out, sent, picks, pick))
    raw = lax.all_to_all(grad_out.reshape(SHARDS, sliver, channels), "tm", 0, 0, tiled=True)
    raw, sent = lax.optimization_barrier((raw, sent))
    swap = [(a, 15 - a) for a in range(8)] + [(8, 0)] + [(a, 16 - a) for a in range(9, 16)]
    swapped = lax.ppermute(sent, "tm", swap)

    late, _ = lax.optimization_barrier((column, raw))
    table = functools.partial(make_table, inner=inner, points=points, factor=factor)
    known = functools.partial(fixed_table, residue=16, inner=inner, points=points, factor=factor)
    residue = 2 * late + pick
    made = [table(residue, transposed=False), table(residue, transposed=True), table(2 * late + 1 - pick, transposed=False)]
    raw, made = lax.optimization_barrier((raw, made))
    picked_tables = made[0] + known(transposed=False) + made[1] + known(transposed=True)
    other_tables = made[2]

    z_tail = (2, RADIX, rows, LANES)

    def expand(raw, picked, first_other, others, name):
        return pl.pallas_call(
            functools.partial(expand_kernel, picked),
            grid=(picked + others,),
            in_specs=[
                pl.BlockSpec((SHARDS, sliver, LANES), lambda c: (0, 0, jnp.where(c < picked, c, c - picked + first_other)))
            ],
            out_specs=pl.BlockSpec((SHARDS, None) + z_tail, lambda c: (0, c, 0, 0, 0, 0)),
            out_shape=jax.ShapeDtypeStruct((SHARDS, picked + others) + z_tail, f32),
            compiler_params=params(),
            cost_estimate=pl.CostEstimate(flops=2**20, bytes_accessed=2**20, transcendentals=0),
            interpret=interpret,
            name=name,
        )(raw)

    first_part = expand(raw, blocks, 0, early, "expand")
    rest = expand(raw, 0, early, blocks - early, "expand_rest")
    swapped, first_part, rest = lax.optimization_barrier((swapped, first_part, rest))
    mirror = lax.all_gather(swapped, "dp", axis=1, tiled=True)
    z_first = lax.all_to_all(first_part, "tm", 0, 0, tiled=True)
    z_first, rest = lax.optimization_barrier((z_first, rest))
    z_rest = lax.all_to_all(rest, "tm", 0, 0, tiled=True)

    def fixed(values):
        return pl.BlockSpec(values.shape, lambda c, s: (0,) * values.ndim, pipeline_mode=pl.Buffered(1))

    def z_spec(shift):
        return pl.BlockSpec((SHARDS, 1) + z_tail, lambda c, s: (0, c + shift, 0, 0, 0, 0))

    saved_shape = (2, None, None, None, length, LANES)
    term_shape = jax.ShapeDtypeStruct((2, 2, 1, length, channels), f32)
    term_block = (2, None, None, length, LANES)
    scratch = [pltpu.VMEM((RADIX, 2, inner, LANES), f32)]

    wide = min(2 * LANES, channels)
    terms, inverted = pl.pallas_call(
        spectrum_kernel,
        grid_spec=pltpu.PrefetchScalarGridSpec(
            num_scalar_prefetch=1,
            grid=(channels // wide,),
            in_specs=[pl.BlockSpec((SHARDS, wide // LANES) + z_tail, lambda c, s: (0, c, 0, 0, 0, 0))]
            + [fixed(table) for table in picked_tables]
            + [
                pl.BlockSpec(saved_shape[:-1] + (wide,), lambda c, s: (0, 0, s[0], 0, 0, c)),
                pl.BlockSpec((2, None, None, length, wide), lambda c, s: (0, s[0], 0, 0, c)),
                pl.BlockSpec((2, length, wide), lambda c, s: (0, 0, c)),
            ],
            out_specs=[
                pl.BlockSpec(term_block[:-1] + (wide,), lambda c, s: (0, s[0], 0, 0, c)),
                pl.BlockSpec((SHARDS, wide // LANES) + z_tail, lambda c, s: (0, c, 0, 0, 0, 0)),
            ],
            scratch_shapes=[pltpu.VMEM((RADIX, 2, inner, wide), f32)],
        ),
        out_shape=[term_shape, jax.ShapeDtypeStruct((SHARDS, blocks) + z_tail, f32)],
        compiler_params=params(),
        cost_estimate=pl.CostEstimate(flops=10**10, bytes_accessed=12 * length * channels * 4, transcendentals=0),
        interpret=interpret,
        name="spectrum",
    )(picks, z_first, *picked_tables, input_spectrum, filter_spectrum, mirror)

    def second(z, at, first_block, count, terms, name):
        return pl.pallas_call(
            other_kernel,
            grid_spec=pltpu.PrefetchScalarGridSpec(
                num_scalar_prefetch=1,
                grid=(count,),
                in_specs=[z_spec(at)]
                + [fixed(table) for table in other_tables]
                + [
                    pl.BlockSpec(saved_shape, lambda c, s: (0, 0, 1 - s[0], 0, 0, c + first_block)),
                    pl.BlockSpec(memory_space=pl.ANY),
                ],
                out_specs=pl.BlockSpec(term_block, lambda c, s: (0, 1 - s[0], 0, 0, c + first_block)),
                scratch_shapes=scratch,
            ),
            out_shape=term_shape,
            input_output_aliases={2 + len(other_tables) + 1: 0},
            compiler_params=params(),
            cost_estimate=pl.CostEstimate(
                flops=2 * 10**9 * count, bytes_accessed=count * 2 * length * LANES * 4 * 3, transcendentals=0
            ),
            interpret=interpret,
            name=name,
        )(picks, z, *other_tables, input_spectrum, terms)

    terms = second(z_first, blocks, 0, early, terms, "other")
    terms, inverted, z_rest = lax.optimization_barrier((terms, inverted, z_rest))
    terms = second(z_rest, 0, early, blocks - early, terms, "other_rest")
    terms, inverted = lax.optimization_barrier((terms, inverted))
    grad_filter = lax.psum_scatter(terms, "dp", scatter_dimension=3, tiled=True)
    landed = lax.all_to_all(inverted, "tm", 0, 0, tiled=True)
    combined = pl.pallas_call(
        combine_kernel,
        grid=(channels // LANES,),
        in_specs=[
            pl.BlockSpec((SHARDS, None) + z_tail, lambda c: (0, c, 0, 0, 0, 0)),
            pl.BlockSpec((SHARDS, sliver, LANES), lambda c: (0, 0, c)),
            pl.BlockSpec((1, LANES), lambda c: (0, c)),
        ],
        out_specs=pl.BlockSpec((SHARDS, sliver, LANES), lambda c: (0, 0, c)),
        out_shape=jax.ShapeDtypeStruct((SHARDS, sliver, channels), f32),
        compiler_params=params(),
        cost_estimate=pl.CostEstimate(flops=400 * length * channels // 16, bytes_accessed=4 * length * channels * 4, transcendentals=0),
        interpret=interpret,
        name="combine",
    )(landed, raw, skip_gain[None])
    back = lax.all_to_all(combined, "tm", 0, 0, tiled=True)
    return (back.reshape(1, length, channels), grad_filter)


def solution(mesh, interpret=False):
    return jax.shard_map(
        functools.partial(on_device, interpret=interpret),
        mesh=mesh,
        in_specs=(
            P("dp", "tm", None),
            P(None, "dp", None, "tm", None, None),
            P(None, None, "tm", None, None),
            P(),
        ),
        out_specs=(P("dp", "tm", None), P(None, None, "tm", "dp", None)),
        check_vma=False,
    )
```

```python
import functools
import math

import jax
import jax.numpy as jnp
import numpy as np
from jax import lax
from jax.experimental import pallas as pl
from jax.experimental.pallas import tpu as pltpu
from jax.sharding import PartitionSpec as P

LANES = 128
SHARDS = 16
RADIX = 4


def weighted(pairs):
    total = None
    for coefficient, value in pairs:
        if abs(coefficient) < 1e-12:
            continue
        if total is None:
            if abs(coefficient - 1.0) < 1e-12:
                total = value
            else:
                total = value * coefficient
        elif abs(coefficient - 1.0) < 1e-12:
            total = total + value
        elif abs(coefficient + 1.0) < 1e-12:
            total = total - value
        else:
            total = total + value * coefficient
    return total


def cos_at(numerator, denominator):
    return math.cos(2.0 * math.pi * (numerator % denominator) / denominator)


def sin_at(numerator, denominator):
    return math.sin(2.0 * math.pi * (numerator % denominator) / denominator)


def residues_of(x):
    total = {n: x[n] + x[16 - n] for n in range(1, 8)}
    diff = {n: x[n] - x[16 - n] for n in range(1, 8)}
    out = {}
    evens, odds = (2, 4, 6), (1, 3, 5, 7)
    for a in range(0, 5):
        even_re = weighted([(1.0, x[0]), (cos_at(8 * a, 16), x[8])] + [(cos_at(n * a, 16), total[n]) for n in evens])
        odd_re = weighted([(cos_at(n * a, 16), total[n]) for n in odds])
        even_im = weighted([(sin_at(n * a, 16), diff[n]) for n in evens])
        odd_im = weighted([(sin_at(n * a, 16), diff[n]) for n in odds])
        if a == 4:
            out[2 * a] = (even_re, -odd_im)
            continue
        re_low, re_high = even_re + odd_re, even_re - odd_re
        if a == 0:
            out[0], out[16] = (re_low, None), (re_high, None)
        else:
            out[2 * a] = (re_low, -(even_im + odd_im))
            out[16 - 2 * a] = (re_high, even_im - odd_im)
    for rho in (1, 3, 5, 7):
        even_re = weighted([(1.0, x[0])] + [(cos_at(n * rho, 32), diff[n]) for n in evens])
        odd_re = weighted([(cos_at(n * rho, 32), diff[n]) for n in odds])
        even_im = weighted([(sin_at(8 * rho, 32), x[8])] + [(sin_at(n * rho, 32), total[n]) for n in evens])
        odd_im = weighted([(sin_at(n * rho, 32), total[n]) for n in odds])
        out[rho] = (even_re + odd_re, -(even_im + odd_im))
        out[16 - rho] = (even_re - odd_re, even_im - odd_im)
    return out


def expand_block(x_ref, out_ref, other):
    groups = x_ref.shape[1] // RADIX // 8

    def step(index, carry):
        t, group = index // groups, index % groups
        row = pl.ds(pl.multiple_of(group * 8, 8), 8)
        values = [x_ref[n, pl.ds(group * 8 * RADIX + t, 8, stride=RADIX), :] for n in range(SHARDS)]
        found = residues_of(values)
        zero = jnp.zeros_like(values[0])
        for a in range(SHARDS):
            rho = 2 * a + ((a >= 8) != other)
            if rho <= 16:
                re, im = found[rho]
                if rho == 0:
                    im = found[16][0]
                elif rho == 16:
                    im = zero
            else:
                re, im = found[32 - rho]
                im = -im
            out_ref[a, 0, t, row, :] = re
            out_ref[a, 1, t, row, :] = im
        return carry

    lax.fori_loop(0, RADIX * groups, step, 0, unroll=True)


def expand_kernel(blocks, x_ref, out_ref):
    @pl.when(pl.program_id(0) < blocks)
    def _():
        expand_block(x_ref, out_ref, False)

    @pl.when(pl.program_id(0) >= blocks)
    def _():
        expand_block(x_ref, out_ref, True)


def turned(value, numerator, denominator):
    re, im = value
    c, s = cos_at(numerator, denominator), sin_at(numerator, denominator)
    if abs(c - s) < 1e-12:
        return (re - im) * c, (re + im) * c
    return re * c - im * s, re * s + im * c


def inverse_four(y):
    (r0, i0), (r1, i1), (r2, i2), (r3, i3) = y
    ar, ai, br, bi = r0 + r2, i0 + i2, r0 - r2, i0 - i2
    cr, ci, dr, di = r1 + r3, i1 + i3, r1 - r3, i1 - i3
    return [(ar + cr, ai + ci), (br - di, bi + dr), (ar - cr, ai - ci), (br + di, bi - dr)]


def conjugate(value):
    return value[0], -value[1]


def times_of(v0, v16, even, odd):
    a, b = v0 + v16, v0 - v16
    f0 = [a + even[4][0], b - even[4][1], a - even[4][0], b + even[4][1]]
    plus = even[2][0] + even[6][0], even[2][1] - even[6][1]
    minus = even[2][0] - even[6][0], even[2][1] + even[6][1]
    corner = turned(minus, 1, 8)
    f1 = [plus[0], corner[0], -plus[1], -corner[1]]
    e0 = [f0[n] + f1[n] for n in range(4)] + [f0[n] - f1[n] for n in range(4)]
    y = inverse_four([even[1], even[5], conjugate(even[7]), conjugate(even[3])])
    c = [y[0]] + [turned(y[m], m, 16) for m in (1, 2, 3)]
    e1 = [c[m][0] for m in range(4)] + [-c[m][1] for m in range(4)]
    y = [conjugate(odd[q]) for q in (1, 5, 9, 13)] + [odd[q] for q in (15, 11, 7, 3)]
    low = inverse_four([y[k] for k in (0, 2, 4, 6)])
    high = inverse_four([y[k] for k in (1, 3, 5, 7)])
    high = [high[0], turned(high[1], 1, 8), (-high[2][1], high[2][0]), turned(high[3], 3, 8)]
    y = [(p[0] + q[0], p[1] + q[1]) for p, q in zip(low, high)] + [(p[0] - q[0], p[1] - q[1]) for p, q in zip(low, high)]
    c = [y[0]] + [turned(y[m], m, 32) for m in range(1, 8)]
    out = [e0[n] + e1[n] + c[n][0] for n in range(8)]
    return out + [e0[n] - e1[n] - c[n][1] for n in range(8)]


def combine_kernel(u_ref, x_ref, gain_ref, out_ref):
    groups = out_ref.shape[1] // RADIX // 8

    def step(index, carry):
        t, group = index // groups, index % groups
        row = pl.ds(pl.multiple_of(group * 8, 8), 8)
        even = {d: (u_ref[d, 0, t, row, :], u_ref[d, 1, t, row, :]) for d in range(1, 8)}
        odd = {31 - 2 * d: (u_ref[d, 0, t, row, :], u_ref[d, 1, t, row, :]) for d in range(8, 16)}
        times = times_of(u_ref[0, 0, t, row, :], u_ref[0, 1, t, row, :], even, odd)
        rows = pl.ds(group * 8 * RADIX + t, 8, stride=RADIX)
        gain = gain_ref[0:1, :]
        for n in range(SHARDS):
            out_ref[n, rows, :] = times[n] + gain * x_ref[n, rows, :]
        return carry

    lax.fori_loop(0, RADIX * groups, step, 0, unroll=True)


dot = functools.partial(jnp.dot, preferred_element_type=jnp.float32)


def halves_of(values):
    high = values.astype(jnp.bfloat16)
    low = (values - high.astype(jnp.float32)).astype(jnp.bfloat16)
    return high, low


def product(tables, t, values):
    high, low = halves_of(values)
    return [
        dot(tables[k][t], high) + (dot(tables[k][t], low) + dot(tables[k + 1][t], high)) for k in (0, 2)
    ]


def turn(parts, sign):
    (r0, i0), (r1, i1), (r2, i2), (r3, i3) = parts
    ar, ai, br, bi = r0 + r2, i0 + i2, r0 - r2, i0 - i2
    cr, ci, dr, di = r1 + r3, i1 + i3, r1 - r3, i1 - i3
    if sign < 0:
        dr, di = -dr, -di
    return (ar + cr, ai + ci), (br + di, bi - dr), (ar - cr, ai - ci), (br - di, bi + dr)


def forward_parts(z_ref, blocks, tables, s_ref):
    inner, lanes = s_ref.shape[2:]
    for t in range(RADIX):
        re = [z_ref[:, c, 0, t].reshape(inner, LANES) for c in blocks]
        im = [z_ref[:, c, 1, t].reshape(inner, LANES) for c in blocks]
        cosine, sine = product(tables, t, jnp.concatenate(re + im, 1))
        s_ref[t, 0] = cosine[:, :lanes] + sine[:, lanes:]
        s_ref[t, 1] = cosine[:, lanes:] - sine[:, :lanes]


def forward_real(z_ref, slot, blocks, tables, s_ref):
    inner = s_ref.shape[2]
    for t in range(RADIX):
        values = jnp.concatenate([z_ref[:, c, slot, t].reshape(inner, LANES) for c in blocks], 1)
        cosine, sine = product(tables, t, values)
        s_ref[t, 0] = cosine
        s_ref[t, 1] = -sine


def rows_at(index):
    return pl.ds(pl.multiple_of(index, 8), 8)


def write_terms(s_ref, row, at, saved_ref, term_ref, re, im):
    a, b = saved_ref[0, at], saved_ref[1, at]
    term_ref[0, at] = a * re + b * im
    term_ref[1, at] = a * im - b * re


def other_kernel(pick_ref, z_ref, *refs):
    tables = refs[:4]
    saved_ref, _, term_ref, s_ref = refs[4:]
    inner = s_ref.shape[2]
    forward_parts(z_ref, [0], tables, s_ref)

    def step(index, carry):
        row = rows_at(index * 8)
        parts = [(s_ref[t, 0, row], s_ref[t, 1, row]) for t in range(RADIX)]
        for q, (re, im) in enumerate(turn(parts, 1)):
            write_terms(s_ref, row, rows_at(q * inner + index * 8), saved_ref, term_ref, re, im)
        return carry

    lax.fori_loop(0, inner // 8, step, 0, unroll=2)


def spectrum_kernel(pick_ref, z_ref, *refs):
    tables, tables16, back, back16 = refs[0:4], refs[4:8], refs[8:12], refs[12:16]
    saved_ref, filt_ref, mirror_ref, term_ref, u_ref, s_ref = refs[16:]
    first = pick_ref[1]
    inner, lanes = s_ref.shape[2:]
    slivers, blocks = u_ref.shape[:2]

    def put(values, slot, t):
        for c in range(blocks):
            u_ref[:, c, slot, t] = values[:, c * LANES : (c + 1) * LANES].reshape(slivers, inner // slivers, LANES)

    def inverse_real(tables, slot):
        for t in range(RADIX):
            total = None
            for k, part in ((0, s_ref[t, 0]), (2, -s_ref[t, 1])):
                high, low = halves_of(part)
                found = dot(tables[k][t], high) + (dot(tables[k][t], low) + dot(tables[k + 1][t], high))
                total = found if total is None else total + found
            put(total, slot, t)

    def middle(weigh, with_terms):
        def step(index, carry):
            row = rows_at(index * 8)
            parts = [(s_ref[t, 0, row], s_ref[t, 1, row]) for t in range(RADIX)]
            back_parts = []
            for q, (re, im) in enumerate(turn(parts, 1)):
                at = rows_at(q * inner + index * 8)
                if with_terms:
                    write_terms(s_ref, row, at, saved_ref, term_ref, re, im)
                a, b = weigh(at)
                back_parts.append((a * re - b * im, a * im + b * re))
            for t, (re, im) in enumerate(turn(back_parts, -1)):
                s_ref[t, 0, row] = re
                s_ref[t, 1, row] = im
            return carry

        lax.fori_loop(0, inner // 8, step, 0, unroll=2)

    @pl.when(first == 0)
    def _():
        forward_parts(z_ref, range(blocks), tables, s_ref)
        middle(lambda at: (filt_ref[0, at] + mirror_ref[0, at], mirror_ref[1, at] - filt_ref[1, at]), True)
        for t in range(RADIX):
            cosine, sine = product(back, t, jnp.concatenate([s_ref[t, 0], s_ref[t, 1]], 1))
            put(cosine[:, :lanes] - sine[:, lanes:], 0, t)
            put(sine[:, :lanes] + cosine[:, lanes:], 1, t)

    @pl.when(first == 1)
    def _():
        forward_real(z_ref, 0, range(blocks), tables, s_ref)
        middle(lambda at: (filt_ref[0, at], -filt_ref[1, at]), True)
        inverse_real(back, 0)
        forward_real(z_ref, 1, range(blocks), tables16, s_ref)
        middle(lambda at: (mirror_ref[0, at], mirror_ref[1, at]), False)
        inverse_real(back16, 1)


def split_table(values):
    high = lax.reduce_precision(values, 8, 7)
    return [high.astype(jnp.bfloat16), (values - high).astype(jnp.bfloat16)]


def base_table(inner, points, transposed):
    time = np.arange(RADIX)[:, None, None] + RADIX * np.arange(inner)[None, None, :]
    angle = 2.0 * np.pi * ((time * 2 * SHARDS * np.arange(inner)[None, :, None]) % points) / points
    if transposed:
        angle = angle.transpose(0, 2, 1)
    return np.cos(angle).astype(np.float32), np.sin(angle).astype(np.float32)


def make_table(residue, inner, points, factor, transposed):
    base_cos, base_sin = base_table(inner, points, transposed)
    time = np.arange(RADIX, dtype=np.int32)[:, None] + RADIX * np.arange(inner, dtype=np.int32)[None, :]
    angle = ((time * residue) % points).astype(jnp.float32) * (2.0 * math.pi / points)
    twist_cos, twist_sin = lax.optimization_barrier((jnp.cos(angle) * factor, jnp.sin(angle) * factor))
    at = (slice(None), slice(None), None) if transposed else (slice(None), None, slice(None))
    twist_cos, twist_sin = twist_cos[at], twist_sin[at]
    cosine = base_cos * twist_cos - base_sin * twist_sin
    sine = base_sin * twist_cos + base_cos * twist_sin
    return split_table(cosine) + split_table(sine)


def fixed_table(residue, inner, points, factor, transposed):
    time = np.arange(RADIX)[:, None, None] + RADIX * np.arange(inner)[None, None, :]
    phase = (time * (residue + 2 * SHARDS * np.arange(inner))[None, :, None]) % points
    if transposed:
        phase = phase.transpose(0, 2, 1)
    found = []
    for values in (np.cos(2.0 * np.pi * phase / points) * factor, np.sin(2.0 * np.pi * phase / points) * factor):
        high = values.astype(np.float32).astype(jnp.bfloat16)
        found += [high, (values - high.astype(np.float64)).astype(jnp.bfloat16)]
    return found


def on_device(grad_out, input_spectrum, filter_spectrum, skip_gain, interpret=False):
    column = lax.axis_index("tm")
    stream = lax.axis_index("dp")
    groups = lax.axis_size("dp")
    _, length, channels = grad_out.shape
    sliver = length // SHARDS
    inner = length // RADIX
    points = 2 * length * SHARDS
    factor = 1.0 / math.sqrt(points)
    params = functools.partial(pltpu.CompilerParams, vmem_limit_bytes=56 * 1024 * 1024)
    f32 = jnp.float32

    pick = (column >= 8).astype(jnp.int32)
    first = (column == 0).astype(jnp.int32)
    picks = jnp.stack([pick, first])

    rows = sliver // RADIX
    blocks = channels // LANES
    early = blocks // 2

    part = length // groups
    filt = filter_spectrum[:, :, 0]
    give = lax.dynamic_index_in_dim(filt, (column < 8).astype(jnp.int32), 1, False)
    sent = lax.rev(lax.dynamic_slice_in_dim(give, (groups - 1 - stream) * part, part, 1), (1,))
    raw = lax.all_to_all(grad_out.reshape(SHARDS, sliver, channels), "tm", 0, 0, tiled=True)
    table = functools.partial(make_table, inner=inner, points=points, factor=factor)
    known = functools.partial(fixed_table, residue=16, inner=inner, points=points, factor=factor)
    residue = 2 * column + pick
    made = [table(residue, transposed=False), table(residue, transposed=True), table(2 * column + 1 - pick, transposed=False)]
    raw, sent, made = lax.optimization_barrier((raw, sent, made))
    swap = [(a, 15 - a) for a in range(8)] + [(8, 0)] + [(a, 16 - a) for a in range(9, 16)]
    swapped = lax.ppermute(sent, "tm", swap)
    picked_tables = made[0] + known(transposed=False) + made[1] + known(transposed=True)
    other_tables = made[2]

    z_tail = (2, RADIX, rows, LANES)

    def expand(raw, picked, first_other, others, name):
        return pl.pallas_call(
            functools.partial(expand_kernel, picked),
            grid=(picked + others,),
            in_specs=[
                pl.BlockSpec((SHARDS, sliver, LANES), lambda c: (0, 0, jnp.where(c < picked, c, c - picked + first_other)))
            ],
            out_specs=pl.BlockSpec((SHARDS, None) + z_tail, lambda c: (0, c, 0, 0, 0, 0)),
            out_shape=jax.ShapeDtypeStruct((SHARDS, picked + others) + z_tail, f32),
            compiler_params=params(),
            cost_estimate=pl.CostEstimate(flops=2**20, bytes_accessed=2**20, transcendentals=0),
            interpret=interpret,
            name=name,
        )(raw)

    first_part = expand(raw, blocks, 0, early, "expand")
    rest = expand(raw, 0, early, blocks - early, "expand_rest")
    swapped, first_part, rest = lax.optimization_barrier((swapped, first_part, rest))
    mirror = lax.all_gather(swapped, "dp", axis=1, tiled=True)
    z_first = lax.all_to_all(first_part, "tm", 0, 0, tiled=True)
    z_first, rest = lax.optimization_barrier((z_first, rest))
    z_rest = lax.all_to_all(rest, "tm", 0, 0, tiled=True)

    def fixed(values):
        return pl.BlockSpec(values.shape, lambda c, s: (0,) * values.ndim, pipeline_mode=pl.Buffered(1))

    def z_spec(shift):
        return pl.BlockSpec((SHARDS, 1) + z_tail, lambda c, s: (0, c + shift, 0, 0, 0, 0))

    saved_shape = (2, None, None, None, length, LANES)
    term_shape = jax.ShapeDtypeStruct((2, 2, 1, length, channels), f32)
    term_block = (2, None, None, length, LANES)
    scratch = [pltpu.VMEM((RADIX, 2, inner, LANES), f32)]

    wide = min(2 * LANES, channels)
    terms, inverted = pl.pallas_call(
        spectrum_kernel,
        grid_spec=pltpu.PrefetchScalarGridSpec(
            num_scalar_prefetch=1,
            grid=(channels // wide,),
            in_specs=[pl.BlockSpec((SHARDS, wide // LANES) + z_tail, lambda c, s: (0, c, 0, 0, 0, 0))]
            + [fixed(table) for table in picked_tables]
            + [
                pl.BlockSpec(saved_shape[:-1] + (wide,), lambda c, s: (0, 0, s[0], 0, 0, c)),
                pl.BlockSpec((2, None, None, length, wide), lambda c, s: (0, s[0], 0, 0, c)),
                pl.BlockSpec((2, length, wide), lambda c, s: (0, 0, c)),
            ],
            out_specs=[
                pl.BlockSpec(term_block[:-1] + (wide,), lambda c, s: (0, s[0], 0, 0, c)),
                pl.BlockSpec((SHARDS, wide // LANES) + z_tail, lambda c, s: (0, c, 0, 0, 0, 0)),
            ],
            scratch_shapes=[pltpu.VMEM((RADIX, 2, inner, wide), f32)],
        ),
        out_shape=[term_shape, jax.ShapeDtypeStruct((SHARDS, blocks) + z_tail, f32)],
        compiler_params=params(),
        cost_estimate=pl.CostEstimate(flops=10**10, bytes_accessed=12 * length * channels * 4, transcendentals=0),
        interpret=interpret,
        name="spectrum",
    )(picks, z_first, *picked_tables, input_spectrum, filter_spectrum, mirror)

    def second(z, at, first_block, count, terms, name):
        return pl.pallas_call(
            other_kernel,
            grid_spec=pltpu.PrefetchScalarGridSpec(
                num_scalar_prefetch=1,
                grid=(count,),
                in_specs=[z_spec(at)]
                + [fixed(table) for table in other_tables]
                + [
                    pl.BlockSpec(saved_shape, lambda c, s: (0, 0, 1 - s[0], 0, 0, c + first_block)),
                    pl.BlockSpec(memory_space=pl.ANY),
                ],
                out_specs=pl.BlockSpec(term_block, lambda c, s: (0, 1 - s[0], 0, 0, c + first_block)),
                scratch_shapes=scratch,
            ),
            out_shape=term_shape,
            input_output_aliases={2 + len(other_tables) + 1: 0},
            compiler_params=params(),
            cost_estimate=pl.CostEstimate(
                flops=2 * 10**9 * count, bytes_accessed=count * 2 * length * LANES * 4 * 3, transcendentals=0
            ),
            interpret=interpret,
            name=name,
        )(picks, z, *other_tables, input_spectrum, terms)

    terms = second(z_first, blocks, 0, early, terms, "other")
    terms, inverted, z_rest = lax.optimization_barrier((terms, inverted, z_rest))
    terms = second(z_rest, 0, early, blocks - early, terms, "other_rest")
    terms, inverted = lax.optimization_barrier((terms, inverted))
    grad_filter = lax.psum_scatter(terms, "dp", scatter_dimension=3, tiled=True)
    landed = lax.all_to_all(inverted, "tm", 0, 0, tiled=True)
    combined = pl.pallas_call(
        combine_kernel,
        grid=(channels // LANES,),
        in_specs=[
            pl.BlockSpec((SHARDS, None) + z_tail, lambda c: (0, c, 0, 0, 0, 0)),
            pl.BlockSpec((SHARDS, sliver, LANES), lambda c: (0, 0, c)),
            pl.BlockSpec((1, LANES), lambda c: (0, c)),
        ],
        out_specs=pl.BlockSpec((SHARDS, sliver, LANES), lambda c: (0, 0, c)),
        out_shape=jax.ShapeDtypeStruct((SHARDS, sliver, channels), f32),
        compiler_params=params(),
        cost_estimate=pl.CostEstimate(flops=400 * length * channels // 16, bytes_accessed=4 * length * channels * 4, transcendentals=0),
        interpret=interpret,
        name="combine",
    )(landed, raw, skip_gain[None])
    back = lax.all_to_all(combined, "tm", 0, 0, tiled=True)
    return (back.reshape(1, length, channels), grad_filter)


def solution(mesh, interpret=False):
    return jax.shard_map(
        functools.partial(on_device, interpret=interpret),
        mesh=mesh,
        in_specs=(
            P("dp", "tm", None),
            P(None, "dp", None, "tm", None, None),
            P(None, None, "tm", None, None),
            P(),
        ),
        out_specs=(P("dp", "tm", None), P(None, None, "tm", "dp", None)),
        check_vma=False,
    )
```

```python
import functools
import math

import jax
import jax.numpy as jnp
import numpy as np
from jax import lax
from jax.experimental import pallas as pl
from jax.experimental.pallas import tpu as pltpu
from jax.sharding import PartitionSpec as P

LANES = 128
SHARDS = 16
RADIX = 4


def weighted(pairs):
    total = None
    for coefficient, value in pairs:
        if abs(coefficient) < 1e-12:
            continue
        if total is None:
            if abs(coefficient - 1.0) < 1e-12:
                total = value
            else:
                total = value * coefficient
        elif abs(coefficient - 1.0) < 1e-12:
            total = total + value
        elif abs(coefficient + 1.0) < 1e-12:
            total = total - value
        else:
            total = total + value * coefficient
    return total


def cos_at(numerator, denominator):
    return math.cos(2.0 * math.pi * (numerator % denominator) / denominator)


def sin_at(numerator, denominator):
    return math.sin(2.0 * math.pi * (numerator % denominator) / denominator)


def residues_of(x):
    total = {n: x[n] + x[16 - n] for n in range(1, 8)}
    diff = {n: x[n] - x[16 - n] for n in range(1, 8)}
    out = {}
    evens, odds = (2, 4, 6), (1, 3, 5, 7)
    for a in range(0, 5):
        even_re = weighted([(1.0, x[0]), (cos_at(8 * a, 16), x[8])] + [(cos_at(n * a, 16), total[n]) for n in evens])
        odd_re = weighted([(cos_at(n * a, 16), total[n]) for n in odds])
        even_im = weighted([(sin_at(n * a, 16), diff[n]) for n in evens])
        odd_im = weighted([(sin_at(n * a, 16), diff[n]) for n in odds])
        if a == 4:
            out[2 * a] = (even_re, -odd_im)
            continue
        re_low, re_high = even_re + odd_re, even_re - odd_re
        if a == 0:
            out[0], out[16] = (re_low, None), (re_high, None)
        else:
            out[2 * a] = (re_low, -(even_im + odd_im))
            out[16 - 2 * a] = (re_high, even_im - odd_im)
    for rho in (1, 3, 5, 7):
        even_re = weighted([(1.0, x[0])] + [(cos_at(n * rho, 32), diff[n]) for n in evens])
        odd_re = weighted([(cos_at(n * rho, 32), diff[n]) for n in odds])
        even_im = weighted([(sin_at(8 * rho, 32), x[8])] + [(sin_at(n * rho, 32), total[n]) for n in evens])
        odd_im = weighted([(sin_at(n * rho, 32), total[n]) for n in odds])
        out[rho] = (even_re + odd_re, -(even_im + odd_im))
        out[16 - rho] = (even_re - odd_re, even_im - odd_im)
    return out


def expand_block(x_ref, out_ref, other):
    groups = x_ref.shape[1] // RADIX // 8

    def step(index, carry):
        t, group = index // groups, index % groups
        row = pl.ds(pl.multiple_of(group * 8, 8), 8)
        values = [x_ref[n, pl.ds(group * 8 * RADIX + t, 8, stride=RADIX), :] for n in range(SHARDS)]
        found = residues_of(values)
        zero = jnp.zeros_like(values[0])
        for a in range(SHARDS):
            rho = 2 * a + ((a >= 8) != other)
            if rho <= 16:
                re, im = found[rho]
                if rho == 0:
                    im = found[16][0]
                elif rho == 16:
                    im = zero
            else:
                re, im = found[32 - rho]
                im = -im
            out_ref[a, 0, t, row, :] = re
            out_ref[a, 1, t, row, :] = im
        return carry

    lax.fori_loop(0, RADIX * groups, step, 0, unroll=True)


def expand_kernel(blocks, x_ref, out_ref):
    @pl.when(pl.program_id(0) < blocks)
    def _():
        expand_block(x_ref, out_ref, False)

    @pl.when(pl.program_id(0) >= blocks)
    def _():
        expand_block(x_ref, out_ref, True)


def times_of(v0, v16, even, odd):
    out = [None] * 16
    ce, se, co, so = {}, {}, {}, {}
    for n in range(0, 5):
        c_even = weighted([(1.0, v0), (1.0 if n % 2 == 0 else -1.0, v16)] + [(cos_at(n * d, 16), even[d][0]) for d in (2, 4, 6)])
        c_odd = weighted([(cos_at(n * d, 16), even[d][0]) for d in (1, 3, 5, 7)])
        s_even = weighted([(sin_at(n * d, 16), even[d][1]) for d in (2, 4, 6)])
        s_odd = weighted([(sin_at(n * d, 16), even[d][1]) for d in (1, 3, 5, 7)])
        if n == 4:
            ce[4], se[4] = c_even, s_odd
        elif n == 0:
            ce[0], ce[8] = c_even + c_odd, c_even - c_odd
        else:
            ce[n], ce[8 - n] = c_even + c_odd, c_even - c_odd
            se[n], se[8 - n] = s_odd + s_even, s_odd - s_even
    re_sum = {q: odd[q][0] + odd[16 - q][0] for q in (1, 3, 5, 7)}
    re_diff = {q: odd[q][0] - odd[16 - q][0] for q in (1, 3, 5, 7)}
    im_sum = {q: odd[q][1] + odd[16 - q][1] for q in (1, 3, 5, 7)}
    im_diff = {q: odd[q][1] - odd[16 - q][1] for q in (1, 3, 5, 7)}
    for n in range(0, 9):
        re_of, im_of = (re_sum, im_diff) if n % 2 == 0 else (re_diff, im_sum)
        co[n] = weighted([(cos_at(n * q, 32), re_of[q]) for q in (1, 3, 5, 7)])
        so[n] = weighted([(sin_at(n * q, 32), im_of[q]) for q in (1, 3, 5, 7)])
    out[0] = ce[0] + co[0]
    out[8] = ce[8] + so[8]
    for n in range(1, 8):
        out[n] = (ce[n] - se[n]) + (co[n] + so[n])
        out[16 - n] = (ce[n] + se[n]) + (so[n] - co[n])
    return out


def combine_kernel(u_ref, x_ref, gain_ref, out_ref):
    groups = out_ref.shape[1] // RADIX // 8

    def step(index, carry):
        t, group = index // groups, index % groups
        row = pl.ds(pl.multiple_of(group * 8, 8), 8)
        even = {d: (u_ref[d, 0, t, row, :], u_ref[d, 1, t, row, :]) for d in range(1, 8)}
        odd = {31 - 2 * d: (u_ref[d, 0, t, row, :], u_ref[d, 1, t, row, :]) for d in range(8, 16)}
        times = times_of(u_ref[0, 0, t, row, :], u_ref[0, 1, t, row, :], even, odd)
        rows = pl.ds(group * 8 * RADIX + t, 8, stride=RADIX)
        gain = gain_ref[0:1, :]
        for n in range(SHARDS):
            out_ref[n, rows, :] = times[n] + gain * x_ref[n, rows, :]
        return carry

    lax.fori_loop(0, RADIX * groups, step, 0, unroll=True)


dot = functools.partial(jnp.dot, preferred_element_type=jnp.float32)


def halves_of(values):
    high = values.astype(jnp.bfloat16)
    low = (values - high.astype(jnp.float32)).astype(jnp.bfloat16)
    return high, low


def product(tables, t, values):
    high, low = halves_of(values)
    return [
        dot(tables[k][t], high) + (dot(tables[k][t], low) + dot(tables[k + 1][t], high)) for k in (0, 2)
    ]


def turn(parts, sign):
    (r0, i0), (r1, i1), (r2, i2), (r3, i3) = parts
    ar, ai, br, bi = r0 + r2, i0 + i2, r0 - r2, i0 - i2
    cr, ci, dr, di = r1 + r3, i1 + i3, r1 - r3, i1 - i3
    if sign < 0:
        dr, di = -dr, -di
    return (ar + cr, ai + ci), (br + di, bi - dr), (ar - cr, ai - ci), (br - di, bi + dr)


def forward_parts(z_ref, blocks, tables, s_ref):
    inner, lanes = s_ref.shape[2:]
    for t in range(RADIX):
        re = [z_ref[:, c, 0, t].reshape(inner, LANES) for c in blocks]
        im = [z_ref[:, c, 1, t].reshape(inner, LANES) for c in blocks]
        cosine, sine = product(tables, t, jnp.concatenate(re + im, 1))
        s_ref[t, 0] = cosine[:, :lanes] + sine[:, lanes:]
        s_ref[t, 1] = cosine[:, lanes:] - sine[:, :lanes]


def forward_real(z_ref, slot, blocks, tables, s_ref):
    inner = s_ref.shape[2]
    for t in range(RADIX):
        values = jnp.concatenate([z_ref[:, c, slot, t].reshape(inner, LANES) for c in blocks], 1)
        cosine, sine = product(tables, t, values)
        s_ref[t, 0] = cosine
        s_ref[t, 1] = -sine


def rows_at(index):
    return pl.ds(pl.multiple_of(index, 8), 8)


def write_terms(s_ref, row, at, saved_ref, term_ref, re, im):
    a, b = saved_ref[0, at], saved_ref[1, at]
    term_ref[0, at] = a * re + b * im
    term_ref[1, at] = a * im - b * re


def other_kernel(pick_ref, z_ref, *refs):
    tables = refs[:4]
    saved_ref, _, term_ref, s_ref = refs[4:]
    inner = s_ref.shape[2]
    forward_parts(z_ref, [0], tables, s_ref)

    def step(index, carry):
        row = rows_at(index * 8)
        parts = [(s_ref[t, 0, row], s_ref[t, 1, row]) for t in range(RADIX)]
        for q, (re, im) in enumerate(turn(parts, 1)):
            write_terms(s_ref, row, rows_at(q * inner + index * 8), saved_ref, term_ref, re, im)
        return carry

    lax.fori_loop(0, inner // 8, step, 0, unroll=2)


def spectrum_kernel(pick_ref, z_ref, *refs):
    tables, tables16, back, back16 = refs[0:4], refs[4:8], refs[8:12], refs[12:16]
    saved_ref, filt_ref, mirror_ref, term_ref, u_ref, s_ref = refs[16:]
    first = pick_ref[1]
    inner, lanes = s_ref.shape[2:]
    slivers, blocks = u_ref.shape[:2]

    def put(values, slot, t):
        for c in range(blocks):
            u_ref[:, c, slot, t] = values[:, c * LANES : (c + 1) * LANES].reshape(slivers, inner // slivers, LANES)

    def inverse_real(tables, slot):
        for t in range(RADIX):
            total = None
            for k, part in ((0, s_ref[t, 0]), (2, -s_ref[t, 1])):
                high, low = halves_of(part)
                found = dot(tables[k][t], high) + (dot(tables[k][t], low) + dot(tables[k + 1][t], high))
                total = found if total is None else total + found
            put(total, slot, t)

    def middle(weigh, with_terms):
        def step(index, carry):
            row = rows_at(index * 8)
            parts = [(s_ref[t, 0, row], s_ref[t, 1, row]) for t in range(RADIX)]
            back_parts = []
            for q, (re, im) in enumerate(turn(parts, 1)):
                at = rows_at(q * inner + index * 8)
                if with_terms:
                    write_terms(s_ref, row, at, saved_ref, term_ref, re, im)
                a, b = weigh(at)
                back_parts.append((a * re - b * im, a * im + b * re))
            for t, (re, im) in enumerate(turn(back_parts, -1)):
                s_ref[t, 0, row] = re
                s_ref[t, 1, row] = im
            return carry

        lax.fori_loop(0, inner // 8, step, 0, unroll=2)

    @pl.when(first == 0)
    def _():
        forward_parts(z_ref, range(blocks), tables, s_ref)
        middle(lambda at: (filt_ref[0, at] + mirror_ref[0, at], mirror_ref[1, at] - filt_ref[1, at]), True)
        for t in range(RADIX):
            cosine, sine = product(back, t, jnp.concatenate([s_ref[t, 0], s_ref[t, 1]], 1))
            put(cosine[:, :lanes] - sine[:, lanes:], 0, t)
            put(sine[:, :lanes] + cosine[:, lanes:], 1, t)

    @pl.when(first == 1)
    def _():
        forward_real(z_ref, 0, range(blocks), tables, s_ref)
        middle(lambda at: (filt_ref[0, at], -filt_ref[1, at]), True)
        inverse_real(back, 0)
        forward_real(z_ref, 1, range(blocks), tables16, s_ref)
        middle(lambda at: (mirror_ref[0, at], mirror_ref[1, at]), False)
        inverse_real(back16, 1)


def split_table(values):
    high = lax.reduce_precision(values, 8, 7)
    return [high.astype(jnp.bfloat16), (values - high).astype(jnp.bfloat16)]


def base_table(inner, points, transposed):
    time = np.arange(RADIX)[:, None, None] + RADIX * np.arange(inner)[None, None, :]
    angle = 2.0 * np.pi * ((time * 2 * SHARDS * np.arange(inner)[None, :, None]) % points) / points
    if transposed:
        angle = angle.transpose(0, 2, 1)
    return np.cos(angle).astype(np.float32), np.sin(angle).astype(np.float32)


def make_table(residue, inner, points, factor, transposed):
    base_cos, base_sin = base_table(inner, points, transposed)
    time = np.arange(RADIX, dtype=np.int32)[:, None] + RADIX * np.arange(inner, dtype=np.int32)[None, :]
    angle = ((time * residue) % points).astype(jnp.float32) * (2.0 * math.pi / points)
    twist_cos, twist_sin = lax.optimization_barrier((jnp.cos(angle) * factor, jnp.sin(angle) * factor))
    at = (slice(None), slice(None), None) if transposed else (slice(None), None, slice(None))
    twist_cos, twist_sin = twist_cos[at], twist_sin[at]
    cosine = base_cos * twist_cos - base_sin * twist_sin
    sine = base_sin * twist_cos + base_cos * twist_sin
    return split_table(cosine) + split_table(sine)


def fixed_table(residue, inner, points, factor, transposed):
    time = np.arange(RADIX)[:, None, None] + RADIX * np.arange(inner)[None, None, :]
    phase = (time * (residue + 2 * SHARDS * np.arange(inner))[None, :, None]) % points
    if transposed:
        phase = phase.transpose(0, 2, 1)
    found = []
    for values in (np.cos(2.0 * np.pi * phase / points) * factor, np.sin(2.0 * np.pi * phase / points) * factor):
        high = values.astype(np.float32).astype(jnp.bfloat16)
        found += [high, (values - high.astype(np.float64)).astype(jnp.bfloat16)]
    return found


def on_device(grad_out, input_spectrum, filter_spectrum, skip_gain, interpret=False):
    column = lax.axis_index("tm")
    stream = lax.axis_index("dp")
    groups = lax.axis_size("dp")
    _, length, channels = grad_out.shape
    sliver = length // SHARDS
    inner = length // RADIX
    points = 2 * length * SHARDS
    factor = 1.0 / math.sqrt(points)
    params = functools.partial(pltpu.CompilerParams, vmem_limit_bytes=56 * 1024 * 1024)
    f32 = jnp.float32

    pick = (column >= 8).astype(jnp.int32)
    first = (column == 0).astype(jnp.int32)
    picks = jnp.stack([pick, first])

    rows = sliver // RADIX
    blocks = channels // LANES
    early = blocks // 2

    lead = (column < 8).astype(jnp.int32)
    grad_out, picks, pick, lead, stream = lax.optimization_barrier((grad_out, picks, pick, lead, stream))
    raw = lax.all_to_all(grad_out.reshape(SHARDS, sliver, channels), "tm", 0, 0, tiled=True)
    raw, lead, stream = lax.optimization_barrier((raw, lead, stream))
    part = length // groups
    filt = filter_spectrum[:, :, 0]
    give = lax.dynamic_index_in_dim(filt, lead, 1, False)
    sent = lax.rev(lax.dynamic_slice_in_dim(give, (groups - 1 - stream) * part, part, 1), (1,))
    swap = [(a, 15 - a) for a in range(8)] + [(8, 0)] + [(a, 16 - a) for a in range(9, 16)]
    swapped = lax.ppermute(sent, "tm", swap)

    late, _ = lax.optimization_barrier((column, raw))
    table = functools.partial(make_table, inner=inner, points=points, factor=factor)
    known = functools.partial(fixed_table, residue=16, inner=inner, points=points, factor=factor)
    residue = 2 * late + pick
    made = [table(residue, transposed=False), table(residue, transposed=True), table(2 * late + 1 - pick, transposed=False)]
    raw, made = lax.optimization_barrier((raw, made))
    picked_tables = made[0] + known(transposed=False) + made[1] + known(transposed=True)
    other_tables = made[2]

    z_tail = (2, RADIX, rows, LANES)

    def expand(raw, picked, first_other, others, name):
        return pl.pallas_call(
            functools.partial(expand_kernel, picked),
            grid=(picked + others,),
            in_specs=[
                pl.BlockSpec((SHARDS, sliver, LANES), lambda c: (0, 0, jnp.where(c < picked, c, c - picked + first_other)))
            ],
            out_specs=pl.BlockSpec((SHARDS, None) + z_tail, lambda c: (0, c, 0, 0, 0, 0)),
            out_shape=jax.ShapeDtypeStruct((SHARDS, picked + others) + z_tail, f32),
            compiler_params=params(),
            cost_estimate=pl.CostEstimate(flops=2**20, bytes_accessed=2**20, transcendentals=0),
            interpret=interpret,
            name=name,
        )(raw)

    first_part = expand(raw, blocks, 0, early, "expand")
    rest = expand(raw, 0, early, blocks - early, "expand_rest")
    swapped, first_part, rest = lax.optimization_barrier((swapped, first_part, rest))
    mirror = lax.all_gather(swapped, "dp", axis=1, tiled=True)
    z_first = lax.all_to_all(first_part, "tm", 0, 0, tiled=True)
    z_first, rest = lax.optimization_barrier((z_first, rest))
    z_rest = lax.all_to_all(rest, "tm", 0, 0, tiled=True)

    def fixed(values):
        return pl.BlockSpec(values.shape, lambda c, s: (0,) * values.ndim, pipeline_mode=pl.Buffered(1))

    def z_spec(shift):
        return pl.BlockSpec((SHARDS, 1) + z_tail, lambda c, s: (0, c + shift, 0, 0, 0, 0))

    saved_shape = (2, None, None, None, length, LANES)
    term_shape = jax.ShapeDtypeStruct((2, 2, 1, length, channels), f32)
    term_block = (2, None, None, length, LANES)
    scratch = [pltpu.VMEM((RADIX, 2, inner, LANES), f32)]

    wide = min(2 * LANES, channels)
    terms, inverted = pl.pallas_call(
        spectrum_kernel,
        grid_spec=pltpu.PrefetchScalarGridSpec(
            num_scalar_prefetch=1,
            grid=(channels // wide,),
            in_specs=[pl.BlockSpec((SHARDS, wide // LANES) + z_tail, lambda c, s: (0, c, 0, 0, 0, 0))]
            + [fixed(table) for table in picked_tables]
            + [
                pl.BlockSpec(saved_shape[:-1] + (wide,), lambda c, s: (0, 0, s[0], 0, 0, c)),
                pl.BlockSpec((2, None, None, length, wide), lambda c, s: (0, s[0], 0, 0, c)),
                pl.BlockSpec((2, length, wide), lambda c, s: (0, 0, c)),
            ],
            out_specs=[
                pl.BlockSpec(term_block[:-1] + (wide,), lambda c, s: (0, s[0], 0, 0, c)),
                pl.BlockSpec((SHARDS, wide // LANES) + z_tail, lambda c, s: (0, c, 0, 0, 0, 0)),
            ],
            scratch_shapes=[pltpu.VMEM((RADIX, 2, inner, wide), f32)],
        ),
        out_shape=[term_shape, jax.ShapeDtypeStruct((SHARDS, blocks) + z_tail, f32)],
        compiler_params=params(),
        cost_estimate=pl.CostEstimate(flops=10**10, bytes_accessed=12 * length * channels * 4, transcendentals=0),
        interpret=interpret,
        name="spectrum",
    )(picks, z_first, *picked_tables, input_spectrum, filter_spectrum, mirror)

    def second(z, at, first_block, count, terms, name):
        return pl.pallas_call(
            other_kernel,
            grid_spec=pltpu.PrefetchScalarGridSpec(
                num_scalar_prefetch=1,
                grid=(count,),
                in_specs=[z_spec(at)]
                + [fixed(table) for table in other_tables]
                + [
                    pl.BlockSpec(saved_shape, lambda c, s: (0, 0, 1 - s[0], 0, 0, c + first_block)),
                    pl.BlockSpec(memory_space=pl.ANY),
                ],
                out_specs=pl.BlockSpec(term_block, lambda c, s: (0, 1 - s[0], 0, 0, c + first_block)),
                scratch_shapes=scratch,
            ),
            out_shape=term_shape,
            input_output_aliases={2 + len(other_tables) + 1: 0},
            compiler_params=params(),
            cost_estimate=pl.CostEstimate(
                flops=2 * 10**9 * count, bytes_accessed=count * 2 * length * LANES * 4 * 3, transcendentals=0
            ),
            interpret=interpret,
            name=name,
        )(picks, z, *other_tables, input_spectrum, terms)

    terms = second(z_first, blocks, 0, early, terms, "other")
    terms, inverted, z_rest = lax.optimization_barrier((terms, inverted, z_rest))
    terms = second(z_rest, 0, early, blocks - early, terms, "other_rest")
    terms, inverted = lax.optimization_barrier((terms, inverted))
    grad_filter = lax.psum_scatter(terms, "dp", scatter_dimension=3, tiled=True)
    landed = lax.all_to_all(inverted, "tm", 0, 0, tiled=True)
    combined = pl.pallas_call(
        combine_kernel,
        grid=(channels // LANES,),
        in_specs=[
            pl.BlockSpec((SHARDS, None) + z_tail, lambda c: (0, c, 0, 0, 0, 0)),
            pl.BlockSpec((SHARDS, sliver, LANES), lambda c: (0, 0, c)),
            pl.BlockSpec((1, LANES), lambda c: (0, c)),
        ],
        out_specs=pl.BlockSpec((SHARDS, sliver, LANES), lambda c: (0, 0, c)),
        out_shape=jax.ShapeDtypeStruct((SHARDS, sliver, channels), f32),
        compiler_params=params(),
        cost_estimate=pl.CostEstimate(flops=400 * length * channels // 16, bytes_accessed=4 * length * channels * 4, transcendentals=0),
        interpret=interpret,
        name="combine",
    )(landed, raw, skip_gain[None])
    back = lax.all_to_all(combined, "tm", 0, 0, tiled=True)
    return (back.reshape(1, length, channels), grad_filter)


def solution(mesh, interpret=False):
    return jax.shard_map(
        functools.partial(on_device, interpret=interpret),
        mesh=mesh,
        in_specs=(
            P("dp", "tm", None),
            P(None, "dp", None, "tm", None, None),
            P(None, None, "tm", None, None),
            P(),
        ),
        out_specs=(P("dp", "tm", None), P(None, None, "tm", "dp", None)),
        check_vma=False,
    )
```

```python
import functools
import math

import jax
import jax.numpy as jnp
import numpy as np
from jax import lax
from jax.experimental import pallas as pl
from jax.experimental.pallas import tpu as pltpu
from jax.sharding import PartitionSpec as P

LANES = 128
SHARDS = 16
RADIX = 4


def weighted(pairs):
    total = None
    for coefficient, value in pairs:
        if abs(coefficient) < 1e-12:
            continue
        if total is None:
            if abs(coefficient - 1.0) < 1e-12:
                total = value
            else:
                total = value * coefficient
        elif abs(coefficient - 1.0) < 1e-12:
            total = total + value
        elif abs(coefficient + 1.0) < 1e-12:
            total = total - value
        else:
            total = total + value * coefficient
    return total


def cos_at(numerator, denominator):
    return math.cos(2.0 * math.pi * (numerator % denominator) / denominator)


def sin_at(numerator, denominator):
    return math.sin(2.0 * math.pi * (numerator % denominator) / denominator)


def residues_of(x):
    total = {n: x[n] + x[16 - n] for n in range(1, 8)}
    diff = {n: x[n] - x[16 - n] for n in range(1, 8)}
    out = {}
    evens, odds = (2, 4, 6), (1, 3, 5, 7)
    for a in range(0, 5):
        even_re = weighted([(1.0, x[0]), (cos_at(8 * a, 16), x[8])] + [(cos_at(n * a, 16), total[n]) for n in evens])
        odd_re = weighted([(cos_at(n * a, 16), total[n]) for n in odds])
        even_im = weighted([(sin_at(n * a, 16), diff[n]) for n in evens])
        odd_im = weighted([(sin_at(n * a, 16), diff[n]) for n in odds])
        if a == 4:
            out[2 * a] = (even_re, -odd_im)
            continue
        re_low, re_high = even_re + odd_re, even_re - odd_re
        if a == 0:
            out[0], out[16] = (re_low, None), (re_high, None)
        else:
            out[2 * a] = (re_low, -(even_im + odd_im))
            out[16 - 2 * a] = (re_high, even_im - odd_im)
    for rho in (1, 3, 5, 7):
        even_re = weighted([(1.0, x[0])] + [(cos_at(n * rho, 32), diff[n]) for n in evens])
        odd_re = weighted([(cos_at(n * rho, 32), diff[n]) for n in odds])
        even_im = weighted([(sin_at(8 * rho, 32), x[8])] + [(sin_at(n * rho, 32), total[n]) for n in evens])
        odd_im = weighted([(sin_at(n * rho, 32), total[n]) for n in odds])
        out[rho] = (even_re + odd_re, -(even_im + odd_im))
        out[16 - rho] = (even_re - odd_re, even_im - odd_im)
    return out


def expand_block(x_ref, out_ref, other):
    groups = x_ref.shape[1] // RADIX // 8

    def step(index, carry):
        t, group = index // groups, index % groups
        row = pl.ds(pl.multiple_of(group * 8, 8), 8)
        values = [x_ref[n, pl.ds(group * 8 * RADIX + t, 8, stride=RADIX), :] for n in range(SHARDS)]
        found = residues_of(values)
        zero = jnp.zeros_like(values[0])
        for a in range(SHARDS):
            rho = 2 * a + ((a >= 8) != other)
            if rho <= 16:
                re, im = found[rho]
                if rho == 0:
                    im = found[16][0]
                elif rho == 16:
                    im = zero
            else:
                re, im = found[32 - rho]
                im = -im
            out_ref[a, 0, t, row, :] = re
            out_ref[a, 1, t, row, :] = im
        return carry

    lax.fori_loop(0, RADIX * groups, step, 0, unroll=True)


def expand_kernel(blocks, x_ref, out_ref):
    @pl.when(pl.program_id(0) < blocks)
    def _():
        expand_block(x_ref, out_ref, False)

    @pl.when(pl.program_id(0) >= blocks)
    def _():
        expand_block(x_ref, out_ref, True)


def times_of(v0, v16, even, odd):
    out = [None] * 16
    ce, se, co, so = {}, {}, {}, {}
    for n in range(0, 5):
        c_even = weighted([(1.0, v0), (1.0 if n % 2 == 0 else -1.0, v16)] + [(cos_at(n * d, 16), even[d][0]) for d in (2, 4, 6)])
        c_odd = weighted([(cos_at(n * d, 16), even[d][0]) for d in (1, 3, 5, 7)])
        s_even = weighted([(sin_at(n * d, 16), even[d][1]) for d in (2, 4, 6)])
        s_odd = weighted([(sin_at(n * d, 16), even[d][1]) for d in (1, 3, 5, 7)])
        if n == 4:
            ce[4], se[4] = c_even, s_odd
        elif n == 0:
            ce[0], ce[8] = c_even + c_odd, c_even - c_odd
        else:
            ce[n], ce[8 - n] = c_even + c_odd, c_even - c_odd
            se[n], se[8 - n] = s_odd + s_even, s_odd - s_even
    re_sum = {q: odd[q][0] + odd[16 - q][0] for q in (1, 3, 5, 7)}
    re_diff = {q: odd[q][0] - odd[16 - q][0] for q in (1, 3, 5, 7)}
    im_sum = {q: odd[q][1] + odd[16 - q][1] for q in (1, 3, 5, 7)}
    im_diff = {q: odd[q][1] - odd[16 - q][1] for q in (1, 3, 5, 7)}
    for n in range(0, 9):
        re_of, im_of = (re_sum, im_diff) if n % 2 == 0 else (re_diff, im_sum)
        co[n] = weighted([(cos_at(n * q, 32), re_of[q]) for q in (1, 3, 5, 7)])
        so[n] = weighted([(sin_at(n * q, 32), im_of[q]) for q in (1, 3, 5, 7)])
    out[0] = ce[0] + co[0]
    out[8] = ce[8] + so[8]
    for n in range(1, 8):
        out[n] = (ce[n] - se[n]) + (co[n] + so[n])
        out[16 - n] = (ce[n] + se[n]) + (so[n] - co[n])
    return out


def combine_kernel(u_ref, x_ref, gain_ref, out_ref):
    groups = out_ref.shape[1] // RADIX // 8

    def step(index, carry):
        t, group = index // groups, index % groups
        row = pl.ds(pl.multiple_of(group * 8, 8), 8)
        even = {d: (u_ref[d, 0, t, row, :], u_ref[d, 1, t, row, :]) for d in range(1, 8)}
        odd = {31 - 2 * d: (u_ref[d, 0, t, row, :], u_ref[d, 1, t, row, :]) for d in range(8, 16)}
        times = times_of(u_ref[0, 0, t, row, :], u_ref[0, 1, t, row, :], even, odd)
        rows = pl.ds(group * 8 * RADIX + t, 8, stride=RADIX)
        gain = gain_ref[0:1, :]
        for n in range(SHARDS):
            out_ref[n, rows, :] = times[n] + gain * x_ref[n, rows, :]
        return carry

    lax.fori_loop(0, RADIX * groups, step, 0, unroll=True)


dot = functools.partial(jnp.dot, preferred_element_type=jnp.float32)


def halves_of(values):
    high = values.astype(jnp.bfloat16)
    low = (values - high.astype(jnp.float32)).astype(jnp.bfloat16)
    return high, low


def product(tables, t, values):
    high, low = halves_of(values)
    return [
        dot(tables[k][t], high) + (dot(tables[k][t], low) + dot(tables[k + 1][t], high)) for k in (0, 2)
    ]


def turn(parts, sign):
    (r0, i0), (r1, i1), (r2, i2), (r3, i3) = parts
    ar, ai, br, bi = r0 + r2, i0 + i2, r0 - r2, i0 - i2
    cr, ci, dr, di = r1 + r3, i1 + i3, r1 - r3, i1 - i3
    if sign < 0:
        dr, di = -dr, -di
    return (ar + cr, ai + ci), (br + di, bi - dr), (ar - cr, ai - ci), (br - di, bi + dr)


def forward_parts(z_ref, blocks, tables, s_ref):
    inner, lanes = s_ref.shape[2:]
    for t in range(RADIX):
        re = [z_ref[:, c, 0, t].reshape(inner, LANES) for c in blocks]
        im = [z_ref[:, c, 1, t].reshape(inner, LANES) for c in blocks]
        cosine, sine = product(tables, t, jnp.concatenate(re + im, 1))
        s_ref[t, 0] = cosine[:, :lanes] + sine[:, lanes:]
        s_ref[t, 1] = cosine[:, lanes:] - sine[:, :lanes]


def forward_real(z_ref, slot, blocks, tables, s_ref):
    inner = s_ref.shape[2]
    for t in range(RADIX):
        values = jnp.concatenate([z_ref[:, c, slot, t].reshape(inner, LANES) for c in blocks], 1)
        cosine, sine = product(tables, t, values)
        s_ref[t, 0] = cosine
        s_ref[t, 1] = -sine


def rows_at(index):
    return pl.ds(pl.multiple_of(index, 8), 8)


def write_terms(s_ref, row, at, saved_ref, term_ref, re, im):
    a, b = saved_ref[0, at], saved_ref[1, at]
    term_ref[0, at] = a * re + b * im
    term_ref[1, at] = a * im - b * re


def other_kernel(pick_ref, z_ref, *refs):
    tables = refs[:4]
    saved_ref, _, term_ref, s_ref = refs[4:]
    inner = s_ref.shape[2]
    forward_parts(z_ref, [0], tables, s_ref)

    def step(index, carry):
        row = rows_at(index * 8)
        parts = [(s_ref[t, 0, row], s_ref[t, 1, row]) for t in range(RADIX)]
        for q, (re, im) in enumerate(turn(parts, 1)):
            write_terms(s_ref, row, rows_at(q * inner + index * 8), saved_ref, term_ref, re, im)
        return carry

    lax.fori_loop(0, inner // 8, step, 0, unroll=2)


def spectrum_kernel(pick_ref, z_ref, *refs):
    tables, tables16, back, back16 = refs[0:4], refs[4:8], refs[8:12], refs[12:16]
    saved_ref, filt_ref, mirror_ref, term_ref, u_ref, s_ref = refs[16:]
    first = pick_ref[1]
    inner, lanes = s_ref.shape[2:]
    slivers, blocks = u_ref.shape[:2]

    def put(values, slot, t):
        for c in range(blocks):
            u_ref[:, c, slot, t] = values[:, c * LANES : (c + 1) * LANES].reshape(slivers, inner // slivers, LANES)

    def inverse_real(tables, slot):
        for t in range(RADIX):
            total = None
            for k, part in ((0, s_ref[t, 0]), (2, -s_ref[t, 1])):
                high, low = halves_of(part)
                found = dot(tables[k][t], high) + (dot(tables[k][t], low) + dot(tables[k + 1][t], high))
                total = found if total is None else total + found
            put(total, slot, t)

    def middle(weigh, with_terms):
        def step(index, carry):
            row = rows_at(index * 8)
            parts = [(s_ref[t, 0, row], s_ref[t, 1, row]) for t in range(RADIX)]
            back_parts = []
            for q, (re, im) in enumerate(turn(parts, 1)):
                at = rows_at(q * inner + index * 8)
                if with_terms:
                    write_terms(s_ref, row, at, saved_ref, term_ref, re, im)
                a, b = weigh(at)
                back_parts.append((a * re - b * im, a * im + b * re))
            for t, (re, im) in enumerate(turn(back_parts, -1)):
                s_ref[t, 0, row] = re
                s_ref[t, 1, row] = im
            return carry

        lax.fori_loop(0, inner // 8, step, 0, unroll=2)

    @pl.when(first == 0)
    def _():
        forward_parts(z_ref, range(blocks), tables, s_ref)
        middle(lambda at: (filt_ref[0, at] + mirror_ref[0, at], mirror_ref[1, at] - filt_ref[1, at]), True)
        for t in range(RADIX):
            cosine, sine = product(back, t, jnp.concatenate([s_ref[t, 0], s_ref[t, 1]], 1))
            put(cosine[:, :lanes] - sine[:, lanes:], 0, t)
            put(sine[:, :lanes] + cosine[:, lanes:], 1, t)

    @pl.when(first == 1)
    def _():
        forward_real(z_ref, 0, range(blocks), tables, s_ref)
        middle(lambda at: (filt_ref[0, at], -filt_ref[1, at]), True)
        inverse_real(back, 0)
        forward_real(z_ref, 1, range(blocks), tables16, s_ref)
        middle(lambda at: (mirror_ref[0, at], mirror_ref[1, at]), False)
        inverse_real(back16, 1)


def split_table(values):
    high = lax.reduce_precision(values, 8, 7)
    return [high.astype(jnp.bfloat16), (values - high).astype(jnp.bfloat16)]


def base_table(inner, points, transposed):
    time = np.arange(RADIX)[:, None, None] + RADIX * np.arange(inner)[None, None, :]
    angle = 2.0 * np.pi * ((time * 2 * SHARDS * np.arange(inner)[None, :, None]) % points) / points
    if transposed:
        angle = angle.transpose(0, 2, 1)
    return np.cos(angle).astype(np.float32), np.sin(angle).astype(np.float32)


def make_table(residue, inner, points, factor, transposed):
    base_cos, base_sin = base_table(inner, points, transposed)
    time = np.arange(RADIX, dtype=np.int32)[:, None] + RADIX * np.arange(inner, dtype=np.int32)[None, :]
    angle = ((time * residue) % points).astype(jnp.float32) * (2.0 * math.pi / points)
    twist_cos, twist_sin = lax.optimization_barrier((jnp.cos(angle) * factor, jnp.sin(angle) * factor))
    at = (slice(None), slice(None), None) if transposed else (slice(None), None, slice(None))
    twist_cos, twist_sin = twist_cos[at], twist_sin[at]
    cosine = base_cos * twist_cos - base_sin * twist_sin
    sine = base_sin * twist_cos + base_cos * twist_sin
    return split_table(cosine) + split_table(sine)


def fixed_table(residue, inner, points, factor, transposed):
    time = np.arange(RADIX)[:, None, None] + RADIX * np.arange(inner)[None, None, :]
    phase = (time * (residue + 2 * SHARDS * np.arange(inner))[None, :, None]) % points
    if transposed:
        phase = phase.transpose(0, 2, 1)
    found = []
    for values in (np.cos(2.0 * np.pi * phase / points) * factor, np.sin(2.0 * np.pi * phase / points) * factor):
        high = values.astype(np.float32).astype(jnp.bfloat16)
        found += [high, (values - high.astype(np.float64)).astype(jnp.bfloat16)]
    return found


def on_device(grad_out, input_spectrum, filter_spectrum, skip_gain, interpret=False):
    column = lax.axis_index("tm")
    stream = lax.axis_index("dp")
    groups = lax.axis_size("dp")
    _, length, channels = grad_out.shape
    sliver = length // SHARDS
    inner = length // RADIX
    points = 2 * length * SHARDS
    factor = 1.0 / math.sqrt(points)
    params = functools.partial(pltpu.CompilerParams, vmem_limit_bytes=56 * 1024 * 1024)
    f32 = jnp.float32

    pick = (column >= 8).astype(jnp.int32)
    first = (column == 0).astype(jnp.int32)
    picks = jnp.stack([pick, first])

    rows = sliver // RADIX
    blocks = channels // LANES
    early = blocks // 2

    lead = (column < 8).astype(jnp.int32)
    grad_out, picks, pick, lead, stream = lax.optimization_barrier((grad_out, picks, pick, lead, stream))
    raw = lax.all_to_all(grad_out.reshape(SHARDS, sliver, channels), "tm", 0, 0, tiled=True)
    raw, lead, stream = lax.optimization_barrier((raw, lead, stream))
    part = length // groups
    filt = filter_spectrum[:, :, 0]
    give = lax.dynamic_index_in_dim(filt, lead, 1, False)
    sent = lax.rev(lax.dynamic_slice_in_dim(give, (groups - 1 - stream) * part, part, 1), (1,))
    swap = [(a, 15 - a) for a in range(8)] + [(8, 0)] + [(a, 16 - a) for a in range(9, 16)]
    swapped = lax.ppermute(sent, "tm", swap)

    late, _ = lax.optimization_barrier((column, raw))
    table = functools.partial(make_table, inner=inner, points=points, factor=factor)
    known = functools.partial(fixed_table, residue=16, inner=inner, points=points, factor=factor)
    residue = 2 * late + pick
    made = [table(residue, transposed=False), table(residue, transposed=True)]
    raw, made = lax.optimization_barrier((raw, made))
    picked_tables = made[0] + known(transposed=False) + made[1] + known(transposed=True)

    z_tail = (2, RADIX, rows, LANES)

    def expand(raw, picked, first_other, others, name):
        return pl.pallas_call(
            functools.partial(expand_kernel, picked),
            grid=(picked + others,),
            in_specs=[
                pl.BlockSpec((SHARDS, sliver, LANES), lambda c: (0, 0, jnp.where(c < picked, c, c - picked + first_other)))
            ],
            out_specs=pl.BlockSpec((SHARDS, None) + z_tail, lambda c: (0, c, 0, 0, 0, 0)),
            out_shape=jax.ShapeDtypeStruct((SHARDS, picked + others) + z_tail, f32),
            compiler_params=params(),
            cost_estimate=pl.CostEstimate(flops=2**20, bytes_accessed=2**20, transcendentals=0),
            interpret=interpret,
            name=name,
        )(raw)

    first_part = expand(raw, blocks, 0, early, "expand")
    rest = expand(raw, 0, early, blocks - early, "expand_rest")
    swapped, first_part, rest = lax.optimization_barrier((swapped, first_part, rest))
    mirror = lax.all_gather(swapped, "dp", axis=1, tiled=True)
    z_first = lax.all_to_all(first_part, "tm", 0, 0, tiled=True)
    z_first, rest = lax.optimization_barrier((z_first, rest))
    z_rest = lax.all_to_all(rest, "tm", 0, 0, tiled=True)
    later, _ = lax.optimization_barrier((column, z_first))
    other_tables = table(2 * later + 1 - pick, transposed=False)

    def fixed(values):
        return pl.BlockSpec(values.shape, lambda c, s: (0,) * values.ndim, pipeline_mode=pl.Buffered(1))

    def z_spec(shift):
        return pl.BlockSpec((SHARDS, 1) + z_tail, lambda c, s: (0, c + shift, 0, 0, 0, 0))

    saved_shape = (2, None, None, None, length, LANES)
    term_shape = jax.ShapeDtypeStruct((2, 2, 1, length, channels), f32)
    term_block = (2, None, None, length, LANES)
    scratch = [pltpu.VMEM((RADIX, 2, inner, LANES), f32)]

    wide = min(2 * LANES, channels)
    terms, inverted = pl.pallas_call(
        spectrum_kernel,
        grid_spec=pltpu.PrefetchScalarGridSpec(
            num_scalar_prefetch=1,
            grid=(channels // wide,),
            in_specs=[pl.BlockSpec((SHARDS, wide // LANES) + z_tail, lambda c, s: (0, c, 0, 0, 0, 0))]
            + [fixed(table) for table in picked_tables]
            + [
                pl.BlockSpec(saved_shape[:-1] + (wide,), lambda c, s: (0, 0, s[0], 0, 0, c)),
                pl.BlockSpec((2, None, None, length, wide), lambda c, s: (0, s[0], 0, 0, c)),
                pl.BlockSpec((2, length, wide), lambda c, s: (0, 0, c)),
            ],
            out_specs=[
                pl.BlockSpec(term_block[:-1] + (wide,), lambda c, s: (0, s[0], 0, 0, c)),
                pl.BlockSpec((SHARDS, wide // LANES) + z_tail, lambda c, s: (0, c, 0, 0, 0, 0)),
            ],
            scratch_shapes=[pltpu.VMEM((RADIX, 2, inner, wide), f32)],
        ),
        out_shape=[term_shape, jax.ShapeDtypeStruct((SHARDS, blocks) + z_tail, f32)],
        compiler_params=params(),
        cost_estimate=pl.CostEstimate(flops=10**10, bytes_accessed=12 * length * channels * 4, transcendentals=0),
        interpret=interpret,
        name="spectrum",
    )(picks, z_first, *picked_tables, input_spectrum, filter_spectrum, mirror)

    def second(z, at, first_block, count, terms, name):
        return pl.pallas_call(
            other_kernel,
            grid_spec=pltpu.PrefetchScalarGridSpec(
                num_scalar_prefetch=1,
                grid=(count,),
                in_specs=[z_spec(at)]
                + [fixed(table) for table in other_tables]
                + [
                    pl.BlockSpec(saved_shape, lambda c, s: (0, 0, 1 - s[0], 0, 0, c + first_block)),
                    pl.BlockSpec(memory_space=pl.ANY),
                ],
                out_specs=pl.BlockSpec(term_block, lambda c, s: (0, 1 - s[0], 0, 0, c + first_block)),
                scratch_shapes=scratch,
            ),
            out_shape=term_shape,
            input_output_aliases={2 + len(other_tables) + 1: 0},
            compiler_params=params(),
            cost_estimate=pl.CostEstimate(
                flops=2 * 10**9 * count, bytes_accessed=count * 2 * length * LANES * 4 * 3, transcendentals=0
            ),
            interpret=interpret,
            name=name,
        )(picks, z, *other_tables, input_spectrum, terms)

    terms = second(z_first, blocks, 0, early, terms, "other")
    terms, inverted, z_rest = lax.optimization_barrier((terms, inverted, z_rest))
    terms = second(z_rest, 0, early, blocks - early, terms, "other_rest")
    terms, inverted = lax.optimization_barrier((terms, inverted))
    grad_filter = lax.psum_scatter(terms, "dp", scatter_dimension=3, tiled=True)
    landed = lax.all_to_all(inverted, "tm", 0, 0, tiled=True)
    combined = pl.pallas_call(
        combine_kernel,
        grid=(channels // LANES,),
        in_specs=[
            pl.BlockSpec((SHARDS, None) + z_tail, lambda c: (0, c, 0, 0, 0, 0)),
            pl.BlockSpec((SHARDS, sliver, LANES), lambda c: (0, 0, c)),
            pl.BlockSpec((1, LANES), lambda c: (0, c)),
        ],
        out_specs=pl.BlockSpec((SHARDS, sliver, LANES), lambda c: (0, 0, c)),
        out_shape=jax.ShapeDtypeStruct((SHARDS, sliver, channels), f32),
        compiler_params=params(),
        cost_estimate=pl.CostEstimate(flops=400 * length * channels // 16, bytes_accessed=4 * length * channels * 4, transcendentals=0),
        interpret=interpret,
        name="combine",
    )(landed, raw, skip_gain[None])
    back = lax.all_to_all(combined, "tm", 0, 0, tiled=True)
    return (back.reshape(1, length, channels), grad_filter)


def solution(mesh, interpret=False):
    return jax.shard_map(
        functools.partial(on_device, interpret=interpret),
        mesh=mesh,
        in_specs=(
            P("dp", "tm", None),
            P(None, "dp", None, "tm", None, None),
            P(None, None, "tm", None, None),
            P(),
        ),
        out_specs=(P("dp", "tm", None), P(None, None, "tm", "dp", None)),
        check_vma=False,
    )
```
